32 devices in a mesh: pb: 16 (over z, x, core), wa: 2 (over y).
Axes of the slice: x: 2, y: 2, z: 4, core: 2. Of those that a mesh axis runs over, the one named last changes fastest.
Arguments:
- psi_val: bfloat16 [16, 8, 1024], P('wa', None, 'pb'), may hold values from -0.796875 to 0.796875
- psi_cond: bfloat16 [16, 12, 1024], P('wa', None, 'pb'), may hold values from -0.796875 to 0.796875
- trials: bfloat16 [16, 1536], P('wa', 'pb'), may hold values from -6 to 6
- screened: bfloat16 [16, 1024, 1024], P('pb', 'wa'), may hold values from -0.1875 to 0.1875
- kmap: int32 [16, 16], P('pb'), may hold values from 0 to 15, each once within a row
Outputs:
- action: float32 [16, 1536], P('wa', 'pb')
The draws below stay inside these ranges and needn't reach their ends.
Inputs may be any that keep to these rules, and one draw needn't show every extreme that they name: Every row of kmap is a permutation of the 16 k-points.
All inputs are finite; a program needn't handle non-finite values.
Results may differ from the reference program's by a relative error of at most 0.005.
Values may be sent and summed in bfloat16 or wider, within the bound.
A program may use at most 64 MiB of HBM per device.

```python
import jax
import jax.numpy as jnp
from jax import lax

V = 8
C = 12
MU = 1024
K = 16
S = 16
Q = 16


def level_of(stream_key, shape, split, smallest, top_value):
    loudness = 1.0
    for position, shards_of in split:
        steps = jax.random.uniform(jax.random.fold_in(jax.random.fold_in(stream_key, 6), position), (shards_of,), jnp.float32, smallest / len(split), top_value / len(split))
        loudness = loudness * jnp.repeat(jnp.exp(steps), shape[position] // shards_of).reshape((-1,) + (1,) * (len(shape) - 1 - position))
    return loudness


def gaussian(key, dims, scale, bound, shards=(), held_as=jnp.bfloat16):
    values = scale * jax.random.normal(key, dims, jnp.float32)
    if shards:
        values = values * level_of(key, dims, shards, -0.22, 0.18)
    return jnp.clip(values, -bound, bound).astype(held_as)


def setup_inputs(seed: int = 0) -> dict:
    streams_of = jax.random.split(jax.random.key(seed), 6)
    psi_val = gaussian(streams_of[0], (K, V, MU), 0.13, 0.796875, ((0, 2), (2, 16)))
    psi_cond = gaussian(streams_of[1], (K, C, MU), 0.13, 0.796875, ((0, 2), (2, 16)))
    trials = gaussian(streams_of[2], (K, S * V * C), 1.0, 6.0, ((0, 2), (1, 16)))
    screened = gaussian(streams_of[3], (Q, MU, MU), MU ** -0.5, 0.1875, ((0, 16), (1, 2)))
    kmap = jax.vmap(lambda own: jax.random.permutation(own, K))(jax.random.split(streams_of[4], Q)).reshape((Q, K)).astype(jnp.int32)
    return dict(psi_val=psi_val, psi_cond=psi_cond, trials=trials, screened=screened, kmap=kmap)


def one_transfer(psi_val, psi_cond, xfull, wq, row):
    hi = lax.Precision.HIGHEST
    valf = psi_val.astype(jnp.float32)
    condf = psi_cond.astype(jnp.float32)
    valp = valf[row]
    condp = condf[row]
    apair = (valf[:, :, None, :] * valp[:, None, :, :]).astype(jnp.bfloat16)
    bpair = (condf[:, :, None, :] * condp[:, None, :, :]).astype(jnp.bfloat16)
    wfull = wq.astype(jnp.float32)
    wa_term = jnp.dot(apair.reshape(-1, MU).astype(jnp.float32), wfull.T, precision=hi).astype(jnp.bfloat16)
    wb_term = jnp.dot(bpair.reshape(-1, MU).astype(jnp.float32), wfull.T, precision=hi).astype(jnp.bfloat16)
    wa_term = wa_term.reshape(K, V, V, MU).astype(jnp.float32)
    wb_term = wb_term.reshape(K, C, C, MU).astype(jnp.float32)
    gmat = jnp.einsum('kcdm,kvum->kcdvu', bpair.astype(jnp.float32), wa_term, precision=hi)
    hmat = jnp.einsum('kcdm,kvum->kcdvu', wb_term, apair.astype(jnp.float32), precision=hi)
    forward = jnp.einsum('kcdvu,ksud->ksvc', gmat, xfull[row], precision=hi)
    backward = jnp.einsum('kdcuv,ksud->ksvc', hmat, xfull, precision=hi)
    return forward + jnp.zeros((K, S, V, C), jnp.float32).at[row].add(backward)


def reference(psi_val, psi_cond, trials, screened, kmap):
    xfull = trials.astype(jnp.float32).reshape(K, S, V, C)

    def step(total, pieces):
        wq, row = pieces
        return total + one_transfer(psi_val, psi_cond, xfull, wq, row.astype(jnp.int32)), None

    total, unused = lax.scan(step, jnp.zeros((K, S, V, C), jnp.float32), (screened, kmap))
    return total.reshape(K, S * V * C)
```

```python
import functools
import math

import jax
import jax.numpy as jnp
from jax import lax
from jax.experimental import pallas as pl
from jax.experimental.pallas import tpu as pltpu
from jax.sharding import PartitionSpec as P

MESH = pl.DeviceIdType.MESH
LANES = 128
PACK = 16
F32 = jnp.float32
BF16 = jnp.bfloat16
NT = (((1,), (1,)), ((), ()))


def up(value, unit):
    return -(-value // unit) * unit


def flip(value, j):
    bit = 1
    while bit <= j:
        if j & bit:
            value = value + bit - 2 * bit * lax.rem(value // bit, 2)
        bit *= 2
    return value


def kernel(dims, kmap_ref, val_hbm, cond_hbm, tri_hbm, w_hbm, out_ref,
           sval, scond, stri, pack_ref, w_ref, slots, val_ref, cond_ref, tri_ref, spread_ref, xt_ref,
           ab_ref, sum_ref, gh_ref, h_ref, res_ref, turn_ref, part_ref, rslots, inv_ref,
           load_sem, w_sem, line_sem, quad_sem, core_sem, hop_send, core_send, give_send, give_recv):
    npb, nwa, klocal, nval, ncond, pts, cols, ntrial, nrows, nx, nz, zc, g = dims
    kcount, points, n = klocal * nwa, pts * npb, npb * nwa
    quads = nx * nwa
    kk_count = klocal // g
    per = LANES // pts
    pairs = nval * nval
    crows = cond_ref.shape[1]
    r = cols // ncond
    spread = nval // r
    width = zc * nx * 2 * pts
    pb, wa = lax.axis_index("pb"), lax.axis_index("wa")
    me = wa * npb + pb
    core, px, pz = lax.rem(pb, 2), lax.rem(pb // 2, nx), pb // (2 * nx)

    def device(z, x, y, c):
        return (z * nx + x) * 2 + c, y

    def there(z, x, y):
        return flip(pz, z), lax.rem(px + x, nx), lax.rem(wa + y, nwa)

    def source(z, x, y):
        return flip(pz, z), lax.rem(px - x + nx, nx), lax.rem(wa - y + nwa, nwa)

    def slot(z, x, y):
        return slots.at[(z * 2 + core) * quads + x * nwa + y]

    others = [(x, y) for x in range(nx) for y in range(nwa) if (x, y) != (0, 0)]
    near = [1] if nz > 1 else []
    far = list(range(2, nz))
    straight = [(0, x, y) for x, y in others] + [(z, 0, 0) for z in near + far]
    straight += [(z, x, y) for z in near for x, y in others]
    twin = device(pz, px, wa, 1 - core)

    barrier = pltpu.get_barrier_semaphore()
    for place in straight:
        pl.semaphore_signal(barrier, inc=1, device_id=device(*there(*place), core), device_id_type=MESH)
    pl.semaphore_signal(barrier, inc=1, device_id=twin, device_id_type=MESH)

    loads = [pltpu.make_async_copy(val_hbm, sval, load_sem.at[0]),
             pltpu.make_async_copy(cond_hbm, scond, load_sem.at[1]),
             pltpu.make_async_copy(tri_hbm, stri, load_sem.at[2])]
    for load in loads:
        load.start()
    wload = pltpu.make_async_copy(w_hbm.at[0], w_ref, w_sem)
    wload.start()
    for load in loads:
        load.wait()

    def beside(pieces):
        have = sum(piece.shape[1] for piece in pieces)
        if have < LANES:
            pieces = pieces + [jnp.zeros((pieces[0].shape[0], LANES - have), F32)]
        return jnp.concatenate(pieces, axis=1) if len(pieces) > 1 else pieces[0]

    for i in range(kk_count):
        pack_ref[i * nval:(i + 1) * nval, :] = beside([sval[j * kk_count + i].astype(F32) for j in range(g)])
        base = kk_count * nval + i * ncond
        pack_ref[base:base + ncond, :] = beside([scond[j * kk_count + i].astype(F32) for j in range(g)])
    base = kk_count * (nval + ncond)
    pack_ref[base:base + klocal, :] = beside([stri[...].astype(F32)])
    if base + klocal < pack_ref.shape[0]:
        pack_ref[base + klocal:, :] = jnp.zeros((pack_ref.shape[0] - base - klocal, LANES), F32)
    slots[(pz * 2 + core) * quads + px * nwa + wa] = pack_ref[...].astype(BF16)

    def copy(held, to, send, recv):
        return pltpu.make_async_remote_copy(
            src_ref=slot(*held), dst_ref=slot(*held), send_sem=send, recv_sem=recv, device_id=to, device_id_type=MESH)

    def wait_for(blocks, send, recv):
        span = slots.at[pl.ds(0, blocks)]
        return pltpu.make_async_remote_copy(
            src_ref=span, dst_ref=span, send_sem=send, recv_sem=recv, device_id=twin, device_id_type=MESH)

    own = source(0, 0, 0)
    pl.semaphore_wait(barrier, len(straight) + 1)
    for z in far:
        copy(own, device(*there(z, 0, 0), core), hop_send, line_sem.at[z]).start()
    for x, y in others:
        copy(own, device(*there(0, x, y), core), hop_send, quad_sem.at[0]).start()
    for z in near:
        for x, y in [(0, 0)] + others:
            copy(own, device(*there(z, x, y), core), hop_send, quad_sem.at[z]).start()
    copy(own, twin, core_send, core_sem.at[0]).start()

    if crows > ncond:
        low = ncond // 8 * 8
        for k in range(kcount):
            cond_ref[k, low:crows, :] = jnp.zeros((crows - low, width), F32)
    for k in range(kcount):
        found = jnp.int32(0)
        for j in range(kcount):
            found = jnp.where(kmap_ref[0, j] == k, j, found)
        inv_ref[k] = found
    tri_ref[...] = jnp.zeros_like(tri_ref)
    for k in range(kcount):
        h_ref[k, ncond * crows:, :] = jnp.zeros((crows * (crows - ncond), LANES), F32)
    wide = ncond * pairs
    lane = lax.broadcasted_iota(jnp.int32, (LANES, wide), 1)
    row = lax.broadcasted_iota(jnp.int32, (LANES, wide), 0)
    spread_ref[...] = jnp.where(lax.rem(lane, nval) * ncond + lane // pairs == row, 1.0, 0.0).astype(BF16)
    wload.wait()

    def across(z, places):
        for x, y in places:
            copy(source(z, x, y), twin, core_send, core_sem.at[z]).start()

    for z in far:
        copy(source(z, 0, 0), device(*there(z, 0, 0), core), hop_send, line_sem.at[z]).wait_recv()
        for x, y in others:
            copy(source(z, 0, 0), device(*there(0, x, y), core), hop_send, quad_sem.at[z]).start()
        across(z, [(0, 0)])
    if others:
        wait_for(len(others), hop_send, quad_sem.at[0]).wait_recv()
        across(0, others)
    for z in near:
        wait_for(quads, hop_send, quad_sem.at[z]).wait_recv()
        across(z, [(0, 0)] + others)

    def far_quads(z):
        if others:
            wait_for(len(others), hop_send, quad_sem.at[z]).wait_recv()
            across(z, others)

    def arrived(z):
        wait_for(quads, core_send, core_sem.at[z]).wait_recv()

    lane_group = lax.broadcasted_iota(jnp.int32, (slots.shape[1], LANES), 1) // pts
    kpad = up(klocal, 8)
    trials_here = zc * nx * 2 // spread

    def unpack(step):
        for w in range(nwa):
            rows = [None] * trials_here
            for t in range(width // LANES):
                at = slice(t * LANES, (t + 1) * LANES)
                blocks = []
                for i in range(t * per, (t + 1) * per):
                    z, x, c = step * zc + i // (nx * 2), i // 2 % nx, i % 2
                    blocks.append(slots[(z * 2 + c) * quads + x * nwa + w].astype(F32))
                    base = kk_count * (nval + ncond)
                    piece = blocks[-1][base:base + klocal]
                    shift = i % spread * cols
                    piece = pltpu.roll(piece, shift, 1) if shift else piece
                    held = rows[i // spread]
                    rows[i // spread] = piece if held is None else held + piece
                for j in range(g):
                    whole = None
                    for i in range(per):
                        shift = (i - j) * pts % LANES
                        moved = pltpu.roll(blocks[i], shift, 1) if shift else blocks[i]
                        whole = moved if whole is None else jnp.where(lane_group == i, moved, whole)
                    for kk in range(kk_count):
                        k = w * klocal + j * kk_count + kk
                        val_ref[k, :, at] = whole[kk * nval:(kk + 1) * nval]
                        base = kk_count * nval + kk * ncond
                        cond_ref[k, 0:ncond, at] = whole[base:base + ncond]
            start = pl.multiple_of((w * ntrial + step * trials_here) * kpad, 8)
            for i in range(trials_here):
                tri_ref[pl.ds(start + i * kpad, klocal), :] = rows[i]
            x = tri_ref[pl.ds(start, trials_here * kpad), :].astype(BF16)
            x = jnp.dot(x, spread_ref[...], preferred_element_type=F32)
            for t in range(wide // LANES):
                xt_ref[t, pl.ds(start, trials_here * kpad), :] = x[:, t * LANES:(t + 1) * LANES]

    local = pl.ds(pl.multiple_of(wa * nrows, nrows), nrows)
    half = lax.broadcasted_iota(jnp.int32, (crows, LANES), 1) < pairs

    def fold(parts):
        pieces = [jnp.where(half, parts[d], parts[d + 1]) for d in range(0, ncond, 2)]
        return jnp.concatenate(pieces, axis=1).astype(BF16)

    def chunk(step, first, last):
        unpack(step)
        start = step * width
        at = pl.ds(pl.multiple_of(start, width), width)

        def one_k(k, carry):
            p = kmap_ref[0, k]
            for t in range(width // LANES):
                tile = slice(t * LANES, (t + 1) * LANES)
                to = pl.ds(pl.multiple_of(start + t * LANES, LANES), LANES)
                mate = val_ref[p, :, tile]
                for v in range(0, nval, 2):
                    two = jnp.concatenate(
                        [val_ref[k, v:v + 1, tile] * mate, val_ref[k, v + 1:v + 2, tile] * mate], axis=0)
                    ab_ref[k, pairs + v * nval:pairs + (v + 2) * nval, to] = two.astype(BF16)
                near_k = val_ref[k, :, tile]
                for u in range(0, nval, 2):
                    two = jnp.concatenate(
                        [val_ref[p, u:u + 1, tile] * near_k, val_ref[p, u + 1:u + 2, tile] * near_k], axis=0)
                    ab_ref[k, u * nval:(u + 2) * nval, to] = two.astype(BF16)
                here = cond_ref[k, :, tile]
                for d in range(ncond):
                    base = 2 * pairs + d * crows
                    ab_ref[k, base:base + crows, to] = (here * cond_ref[p, d:d + 1, tile]).astype(BF16)
            part = lax.dot_general(ab_ref[k, pairs:, at], w_ref[:, at], NT, preferred_element_type=F32)
            if not first:
                part = part + sum_ref[k]
            if not last:
                sum_ref[k] = part
                return carry
            part = part.astype(BF16)
            twice = jnp.concatenate([part[:pairs]] * 2, axis=0)
            gmat = lax.dot_general(ab_ref[k, 2 * pairs:, local], twice, NT, preferred_element_type=F32)
            a = ab_ref[k, :pairs, local]
            hmat = lax.dot_general(part[pairs:], jnp.concatenate([a, a], axis=0), NT, preferred_element_type=F32)
            gh_ref[k, 0:crows] = fold([gmat[d * crows:(d + 1) * crows] for d in range(ncond)])
            h_ref[k, 0:ncond * crows] = hmat
            gh_ref[k, crows:2 * crows] = fold([h_ref[k, pl.ds(d, crows, stride=crows), :] for d in range(ncond)])
            return carry

        lax.fori_loop(0, kcount, one_k, 0, unroll=2)

    if zc == 1:
        order = [0] + near + far
        for i, z in enumerate(order):
            if i == len(order) - len(far):
                for later in far:
                    far_quads(later)
            arrived(z)
            chunk(flip(pz, z), i == 0, i == len(order) - 1)
    else:
        for z in far:
            far_quads(z)
        for z in range(nz):
            arrived(z)
        chunk(0, True, False)

        def some(step, carry):
            chunk(step, False, False)
            return carry

        lax.fori_loop(1, nz // zc - 1, some, 0)
        chunk(nz // zc - 1, False, True)

    which = lax.rem(lax.broadcasted_iota(jnp.int32, (ntrial, wide), 1) // nval, nval)
    spots = [jnp.where(which == v, 1.0, 0.0).astype(BF16) for v in range(nval)]

    def one_p(p, carry):
        w, kl = p // klocal, lax.rem(p, klocal)
        x = jnp.concatenate([xt_ref[t, pl.ds(w * ntrial * kpad + kl, ntrial, stride=kpad), :]
                             for t in range(wide // LANES)], axis=1).astype(BF16)
        x = jnp.concatenate([x * spots[v] for v in range(nval)], axis=0)
        both = jnp.concatenate([gh_ref[inv_ref[p], 0:crows], gh_ref[p, crows:2 * crows]], axis=0)
        res_ref[p] = lax.dot_general(both, x, NT, preferred_element_type=F32)
        return carry

    lax.fori_loop(0, kcount, one_p, 0, unroll=2)

    def give(to, mine):
        return pltpu.make_async_remote_copy(
            src_ref=part_ref.at[to], dst_ref=rslots.at[mine], send_sem=give_send, recv_sem=give_recv,
            device_id=(lax.rem(to, npb), to // npb), device_id_type=MESH)

    for w in range(nwa):
        rows = [res_ref[kmap_ref[0, k], 0:crows] + res_ref[inv_ref[k], crows:2 * crows]
                for k in reversed(range(w * klocal, (w + 1) * klocal))]
        if klocal * crows < LANES:
            rows.append(jnp.zeros((LANES - klocal * crows, nval * ntrial), F32))
        turn_ref[w] = jnp.concatenate(rows, axis=0).T
        for i in range(npb):
            s, v0 = i * r // nval, i * r % nval
            part_ref[w * npb + i] = turn_ref[w, pl.ds(v0 * ntrial + s, r, stride=ntrial), :]
    rslots[me] = part_ref[me]

    def send(j, carry):
        give(lax.rem(me + j, n), me).start()
        return carry

    lax.fori_loop(1, n, send, 0)
    every = pltpu.make_async_remote_copy(
        src_ref=part_ref.at[pl.ds(0, n - 1)], dst_ref=rslots.at[pl.ds(0, n - 1)], send_sem=give_send,
        recv_sem=give_recv, device_id=twin, device_id_type=MESH)
    wait_for(len(straight) + len(far) * len(others), hop_send, line_sem.at[0]).wait_send()
    wait_for(nz * quads, core_send, line_sem.at[0]).wait_send()
    every.wait_recv()
    total = jnp.sum(rslots[...], axis=0)
    lanes = lax.broadcasted_iota(jnp.int32, (klocal, LANES), 1)
    result = jnp.zeros((klocal, LANES), F32)
    for v in range(r):
        shift = (v * ncond - (klocal - 1) * crows) % LANES
        moved = pltpu.roll(jnp.broadcast_to(total[v:v + 1], (klocal, LANES)), 0, 1, stride=crows, stride_axis=0)
        moved = pltpu.roll(moved, shift, 1) if shift else moved
        keep = jnp.logical_and(lanes >= v * ncond, lanes < (v + 1) * ncond)
        result = jnp.where(keep, moved, result)
    out_ref[...] = result[:, :cols]
    every.wait_send()


def shards(npb, nwa, psi_val, psi_cond, trials, screened, kmap):
    klocal, nval, pts = psi_val.shape
    ncond = psi_cond.shape[1]
    cols = trials.shape[1]
    kcount, points, n = klocal * nwa, pts * npb, npb * nwa
    ntrial = cols * npb // (nval * ncond)
    nrows = screened.shape[1]
    nx = 2 if npb % 4 == 0 else 1
    nz = npb // (2 * nx)
    zc = max(1, LANES // (nx * 2 * pts))
    g = math.gcd(klocal, LANES // pts)
    vmem = pl.BlockSpec(memory_space=pltpu.VMEM)
    smem = pl.BlockSpec(memory_space=pltpu.SMEM)
    anywhere = pl.BlockSpec(memory_space=pl.ANY)
    prow = up(klocal // g * (nval + ncond) + klocal, PACK)
    r = cols // ncond
    crows = up(ncond, PACK)
    pairs = nval * nval
    rows = pairs + ncond * crows
    wide = ncond * pairs
    width = zc * nx * 2 * pts
    kpad = up(klocal, 8)
    dims = (npb, nwa, klocal, nval, ncond, pts, cols, ntrial, nrows, nx, nz, zc, g)
    dma = pltpu.SemaphoreType.DMA
    return pl.pallas_call(
        functools.partial(kernel, dims),
        out_shape=jax.ShapeDtypeStruct((klocal, cols), F32),
        in_specs=[smem] + [anywhere] * 4, out_specs=vmem,
        scratch_shapes=[
            pltpu.VMEM(psi_val.shape, BF16),
            pltpu.VMEM(psi_cond.shape, BF16),
            pltpu.VMEM(trials.shape, BF16),
            pltpu.VMEM((prow, LANES), F32),
            pltpu.VMEM((nrows, points), BF16),
            pltpu.VMEM((n, prow, LANES), BF16),
            pltpu.VMEM((kcount, nval, width), F32),
            pltpu.VMEM((kcount, crows, width), F32),
            pltpu.VMEM((nwa * ntrial * kpad, LANES), F32),
            pltpu.VMEM((LANES, wide), BF16),
            pltpu.VMEM((wide // LANES, nwa * ntrial * kpad, LANES), F32),
            pltpu.VMEM((kcount, pairs + rows, points), BF16),
            pltpu.VMEM((kcount, rows, nrows), F32),
            pltpu.VMEM((kcount, 2 * crows, wide), BF16),
            pltpu.VMEM((kcount, crows * crows, LANES), F32),
            pltpu.VMEM((kcount, 2 * crows, nval * ntrial), F32),
            pltpu.VMEM((nwa, nval * ntrial, LANES), F32),
            pltpu.VMEM((n, r, LANES), F32),
            pltpu.VMEM((n, r, LANES), F32),
            pltpu.SMEM((kcount,), jnp.int32),
            dma((3,)), dma, dma((nz,)), dma((nz,)), dma((nz,)), dma, dma, dma, dma,
        ],
        compiler_params=pltpu.CompilerParams(
            collective_id=0, has_side_effects=True, vmem_limit_bytes=44 * 1024 * 1024),
        name="bethe",
    )(kmap, psi_val, psi_cond, trials, screened)


def solution(mesh):
    in_specs = (
        P("wa", None, "pb"),
        P("wa", None, "pb"),
        P("wa", "pb"),
        P("pb", "wa", None),
        P("pb", None),
    )
    body = functools.partial(shards, mesh.shape["pb"], mesh.shape["wa"])
    return jax.shard_map(body, mesh=mesh, in_specs=in_specs, out_specs=P("wa", "pb"), check_vma=False)
```

```python
import functools
import math

import jax
import jax.numpy as jnp
from jax import lax
from jax.experimental import pallas as pl
from jax.experimental.pallas import tpu as pltpu
from jax.sharding import PartitionSpec as P

MESH = pl.DeviceIdType.MESH
LANES = 128
PACK = 16
F32 = jnp.float32
BF16 = jnp.bfloat16
NT = (((1,), (1,)), ((), ()))


def up(value, unit):
    return -(-value // unit) * unit


def flip(value, j):
    bit = 1
    while bit <= j:
        if j & bit:
            value = value + bit - 2 * bit * lax.rem(value // bit, 2)
        bit *= 2
    return value


def kernel(dims, kmap_ref, val_hbm, cond_hbm, tri_hbm, w_hbm, out_ref,
           sval, scond, stri, pack_ref, w_ref, slots, val_ref, cond_ref, tri_ref, spread_ref, xt_ref,
           b_ref, sum_ref, right_ref, gh_ref, h_ref, res_ref, turn_ref, part_ref, rslots, inv_ref,
           load_sem, w_sem, line_sem, quad_sem, core_sem, hop_send, core_send, give_send, give_recv):
    npb, nwa, klocal, nval, ncond, pts, cols, ntrial, nrows, nx, nz, g = dims
    kcount, points, n = klocal * nwa, pts * npb, npb * nwa
    quads = nx * nwa
    kk_count = klocal // g
    per = LANES // pts
    pairs = nval * nval
    crows = cond_ref.shape[1]
    r = cols // ncond
    spread = nval // r
    width = points // 2
    deep = nz // 2
    pb, wa = lax.axis_index("pb"), lax.axis_index("wa")
    me = wa * npb + pb
    core, px, pz = lax.rem(pb, 2), lax.rem(pb // 2, nx), pb // (2 * nx)

    def device(z, x, y, c):
        return (z * nx + x) * 2 + c, y

    def there(z, x, y):
        return flip(pz, z), lax.rem(px + x, nx), lax.rem(wa + y, nwa)

    def source(z, x, y):
        return flip(pz, z), lax.rem(px - x + nx, nx), lax.rem(wa - y + nwa, nwa)

    def slot(z, x, y):
        return slots.at[(z * 2 + core) * quads + x * nwa + y]

    others = [(x, y) for x in range(nx) for y in range(nwa) if (x, y) != (0, 0)]
    near = list(range(1, nz // 2))
    far = list(range(nz // 2, nz))
    straight = [(0, x, y) for x, y in others] + [(z, 0, 0) for z in near + far]
    straight += [(z, x, y) for z in near for x, y in others]
    twin = device(pz, px, wa, 1 - core)

    barrier = pltpu.get_barrier_semaphore()
    for place in straight:
        pl.semaphore_signal(barrier, inc=1, device_id=device(*there(*place), core), device_id_type=MESH)
    pl.semaphore_signal(barrier, inc=1, device_id=twin, device_id_type=MESH)

    loads = [pltpu.make_async_copy(val_hbm, sval, load_sem.at[0]),
             pltpu.make_async_copy(cond_hbm, scond, load_sem.at[1]),
             pltpu.make_async_copy(tri_hbm, stri, load_sem.at[2])]
    for load in loads:
        load.start()
    wload = pltpu.make_async_copy(w_hbm.at[0], w_ref, w_sem)
    wload.start()
    for load in loads:
        load.wait()

    def beside(pieces):
        have = sum(piece.shape[1] for piece in pieces)
        if have < LANES:
            pieces = pieces + [jnp.zeros((pieces[0].shape[0], LANES - have), F32)]
        return jnp.concatenate(pieces, axis=1) if len(pieces) > 1 else pieces[0]

    for i in range(kk_count):
        pack_ref[i * nval:(i + 1) * nval, :] = beside([sval[j * kk_count + i].astype(F32) for j in range(g)])
        base = kk_count * nval + i * ncond
        pack_ref[base:base + ncond, :] = beside([scond[j * kk_count + i].astype(F32) for j in range(g)])
    base = kk_count * (nval + ncond)
    pack_ref[base:base + klocal, :] = beside([stri[...].astype(F32)])
    if base + klocal < pack_ref.shape[0]:
        pack_ref[base + klocal:, :] = jnp.zeros((pack_ref.shape[0] - base - klocal, LANES), F32)
    slots[(pz * 2 + core) * quads + px * nwa + wa] = pack_ref[...].astype(BF16)

    def copy(held, to, send, recv):
        return pltpu.make_async_remote_copy(
            src_ref=slot(*held), dst_ref=slot(*held), send_sem=send, recv_sem=recv, device_id=to, device_id_type=MESH)

    def wait_for(blocks, send, recv):
        span = slots.at[pl.ds(0, blocks)]
        return pltpu.make_async_remote_copy(
            src_ref=span, dst_ref=span, send_sem=send, recv_sem=recv, device_id=twin, device_id_type=MESH)

    own = source(0, 0, 0)
    pl.semaphore_wait(barrier, len(straight) + 1)
    for z in far:
        copy(own, device(*there(z, 0, 0), core), hop_send, line_sem.at[z]).start()
    for x, y in others:
        copy(own, device(*there(0, x, y), core), hop_send, quad_sem.at[0]).start()
    for z in near:
        for x, y in [(0, 0)] + others:
            copy(own, device(*there(z, x, y), core), hop_send, quad_sem.at[z]).start()
    copy(own, twin, core_send, core_sem.at[0]).start()

    if crows > ncond:
        low = ncond // 8 * 8
        for k in range(kcount):
            cond_ref[k, low:crows, :] = jnp.zeros((crows - low, width), F32)
    for k in range(kcount):
        found = jnp.int32(0)
        for j in range(kcount):
            found = jnp.where(kmap_ref[0, j] == k, j, found)
        inv_ref[k] = found
    tri_ref[...] = jnp.zeros_like(tri_ref)
    for k in range(kcount):
        h_ref[k, ncond * crows:, :] = jnp.zeros((crows * (crows - ncond), LANES), F32)
        right_ref[k, 0:pairs, :] = jnp.zeros((pairs, points), BF16)
    wide = ncond * pairs
    lane = lax.broadcasted_iota(jnp.int32, (LANES, wide), 1)
    row = lax.broadcasted_iota(jnp.int32, (LANES, wide), 0)
    spread_ref[...] = jnp.where(lax.rem(lane, nval) * ncond + lane // pairs == row, 1.0, 0.0).astype(BF16)
    wload.wait()

    def across(z, places):
        for x, y in places:
            copy(source(z, x, y), twin, core_send, core_sem.at[z]).start()

    for z in far:
        copy(source(z, 0, 0), device(*there(z, 0, 0), core), hop_send, line_sem.at[z]).wait_recv()
        for x, y in others:
            copy(source(z, 0, 0), device(*there(0, x, y), core), hop_send, quad_sem.at[z]).start()
        across(z, [(0, 0)])
    if others:
        wait_for(len(others), hop_send, quad_sem.at[0]).wait_recv()
        across(0, others)
    for z in near:
        wait_for(quads, hop_send, quad_sem.at[z]).wait_recv()
        across(z, [(0, 0)] + others)

    def far_quads(z):
        if others:
            wait_for(len(others), hop_send, quad_sem.at[z]).wait_recv()
            across(z, others)

    def arrived(z):
        wait_for(quads, core_send, core_sem.at[z]).wait_recv()

    lane_group = lax.broadcasted_iota(jnp.int32, (slots.shape[1], LANES), 1) // pts
    kpad = up(klocal, 8)
    trials_here = deep * nx * 2 // spread

    def unpack(side):
        for w in range(nwa):
            rows = [None] * trials_here
            for t in range(width // LANES):
                at = slice(t * LANES, (t + 1) * LANES)
                whole_at = pl.ds(pl.multiple_of(side * width + t * LANES, LANES), LANES)
                blocks = []
                for i in range(t * per, (t + 1) * per):
                    z, x, c = side * deep + i // (nx * 2), i // 2 % nx, i % 2
                    blocks.append(slots[(z * 2 + c) * quads + x * nwa + w].astype(F32))
                    base = kk_count * (nval + ncond)
                    piece = blocks[-1][base:base + klocal]
                    shift = i % spread * cols
                    piece = pltpu.roll(piece, shift, 1) if shift else piece
                    held = rows[i // spread]
                    rows[i // spread] = piece if held is None else held + piece
                for j in range(g):
                    whole = None
                    for i in range(per):
                        shift = (i - j) * pts % LANES
                        moved = pltpu.roll(blocks[i], shift, 1) if shift else blocks[i]
                        whole = moved if whole is None else jnp.where(lane_group == i, moved, whole)
                    for kk in range(kk_count):
                        k = w * klocal + j * kk_count + kk
                        val_ref[k, :, whole_at] = whole[kk * nval:(kk + 1) * nval]
                        base = kk_count * nval + kk * ncond
                        cond_ref[k, 0:ncond, at] = whole[base:base + ncond]
            start = pl.multiple_of((w * ntrial + side * trials_here) * kpad, 8)
            for i in range(trials_here):
                tri_ref[pl.ds(start + i * kpad, klocal), :] = rows[i]
            x = tri_ref[pl.ds(start, trials_here * kpad), :].astype(BF16)
            x = jnp.dot(x, spread_ref[...], preferred_element_type=F32)
            for t in range(wide // LANES):
                xt_ref[t, pl.ds(start, trials_here * kpad), :] = x[:, t * LANES:(t + 1) * LANES]

    local = pl.ds(pl.multiple_of(wa * nrows, nrows), nrows)
    half = lax.broadcasted_iota(jnp.int32, (crows, LANES), 1) < pairs
    block = math.gcd(kcount, max(1, 256 // pairs))

    def products(one, two, at):
        parts = []
        mate = val_ref[two, :, at]
        for v in range(0, nval, 2):
            both = jnp.concatenate([val_ref[one, v:v + 1, at] * mate, val_ref[one, v + 1:v + 2, at] * mate], axis=0)
            parts.append(both.astype(BF16))
        return jnp.concatenate(parts, axis=0)

    def build(k, side):
        p = kmap_ref[0, k]
        for t in range(width // LANES):
            tile = slice(t * LANES, (t + 1) * LANES)
            to = pl.ds(pl.multiple_of(side * width + t * LANES, LANES), LANES)
            here = cond_ref[k, :, tile]
            for d in range(ncond):
                b_ref[k, d * crows:(d + 1) * crows, to] = (here * cond_ref[p, d:d + 1, tile]).astype(BF16)

    def rows_of(b, side):
        whole = []
        for i in range(block):
            k = b * block + i
            whole.append(jnp.concatenate(
                [products(k, kmap_ref[0, k], pl.ds(pl.multiple_of(side * width + t, LANES), LANES))
                 for t in range(0, width, LANES)], axis=1))
        at = pl.ds(pl.multiple_of(side * width, LANES), width)
        return lax.dot_general(jnp.concatenate(whole, axis=0), w_ref[:, at], NT, preferred_element_type=F32)

    def early(side):
        unpack(side)

        def step(b, carry):
            sum_ref[b] = rows_of(b, side)
            for i in range(block):
                build(b * block + i, side)
            return carry

        lax.fori_loop(0, kcount // block, step, 0)

    def late(side):
        unpack(side)

        def step(b, carry):
            left = (sum_ref[b] + rows_of(b, side)).astype(BF16)
            whole = []
            for i in range(block):
                k = b * block + i
                right_ref[k, 0:pairs, local] = left[i * pairs:(i + 1) * pairs]
                whole.append(jnp.concatenate(
                    [products(kmap_ref[0, k], k, pl.ds(pl.multiple_of(wa * nrows + t, LANES), LANES))
                     for t in range(0, nrows, LANES)], axis=1))
                build(k, side)
            turned = jnp.dot(jnp.concatenate(whole, axis=0), w_ref[...], preferred_element_type=F32).astype(BF16)
            for i in range(block):
                right_ref[b * block + i, pairs:2 * pairs, :] = turned[i * pairs:(i + 1) * pairs]
            return carry

        lax.fori_loop(0, kcount // block, step, 0)

        def one_k(k, carry):
            both = lax.dot_general(b_ref[k], right_ref[k], NT, preferred_element_type=F32)
            h_ref[k, 0:ncond * crows] = both
            g_parts = [both[d * crows:(d + 1) * crows] for d in range(ncond)]
            h_parts = [h_ref[k, pl.ds(d, crows, stride=crows), :] for d in range(ncond)]
            for d in range(0, ncond, 2):
                at = slice(d * pairs, (d + 2) * pairs)
                gh_ref[k, 0:crows, at] = jnp.where(half, g_parts[d], pltpu.roll(g_parts[d + 1], pairs, 1)).astype(BF16)
                gh_ref[k, crows:, at] = jnp.where(half, pltpu.roll(h_parts[d], pairs, 1), h_parts[d + 1]).astype(BF16)
            return carry

        lax.fori_loop(0, kcount, one_k, 0, unroll=math.gcd(kcount, 8))

    side = pz // deep
    for z in [0] + near:
        arrived(z)
    early(side)
    for z in far:
        far_quads(z)
    for z in far:
        arrived(z)
    late(1 - side)

    which = lax.rem(lax.broadcasted_iota(jnp.int32, (ntrial, wide), 1) // nval, nval)
    spots = [jnp.where(which == v, 1.0, 0.0).astype(BF16) for v in range(nval)]

    def one_p(p, carry):
        w, kl = p // klocal, lax.rem(p, klocal)
        x = jnp.concatenate([xt_ref[t, pl.ds(w * ntrial * kpad + kl, ntrial, stride=kpad), :]
                             for t in range(wide // LANES)], axis=1).astype(BF16)
        x = jnp.concatenate([x * spots[v] for v in range(nval)], axis=0)
        both = jnp.concatenate([gh_ref[inv_ref[p], 0:crows], gh_ref[p, crows:2 * crows]], axis=0)
        res_ref[p] = lax.dot_general(both, x, NT, preferred_element_type=F32)
        return carry

    lax.fori_loop(0, kcount, one_p, 0, unroll=math.gcd(kcount, 8))

    def give(to, mine):
        return pltpu.make_async_remote_copy(
            src_ref=part_ref.at[to], dst_ref=rslots.at[mine], send_sem=give_send, recv_sem=give_recv,
            device_id=(lax.rem(to, npb), to // npb), device_id_type=MESH)

    for w in range(nwa):
        rows = [res_ref[kmap_ref[0, k], 0:crows] + res_ref[inv_ref[k], crows:2 * crows]
                for k in reversed(range(w * klocal, (w + 1) * klocal))]
        if klocal * crows < LANES:
            rows.append(jnp.zeros((LANES - klocal * crows, nval * ntrial), F32))
        turn_ref[w] = jnp.concatenate(rows, axis=0).T
        for i in range(npb):
            s, v0 = i * r // nval, i * r % nval
            part_ref[w * npb + i] = turn_ref[w, pl.ds(v0 * ntrial + s, r, stride=ntrial), :]
    rslots[me] = part_ref[me]

    def send(j, carry):
        give(lax.rem(me + j, n), me).start()
        return carry

    lax.fori_loop(1, n, send, 0)
    every = pltpu.make_async_remote_copy(
        src_ref=part_ref.at[pl.ds(0, n - 1)], dst_ref=rslots.at[pl.ds(0, n - 1)], send_sem=give_send,
        recv_sem=give_recv, device_id=twin, device_id_type=MESH)
    wait_for(len(straight) + len(far) * len(others), hop_send, line_sem.at[0]).wait_send()
    wait_for(nz * quads, core_send, line_sem.at[0]).wait_send()
    every.wait_recv()
    total = jnp.sum(rslots[...], axis=0)
    lanes = lax.broadcasted_iota(jnp.int32, (klocal, LANES), 1)
    result = jnp.zeros((klocal, LANES), F32)
    for v in range(r):
        shift = (v * ncond - (klocal - 1) * crows) % LANES
        moved = pltpu.roll(jnp.broadcast_to(total[v:v + 1], (klocal, LANES)), 0, 1, stride=crows, stride_axis=0)
        moved = pltpu.roll(moved, shift, 1) if shift else moved
        keep = jnp.logical_and(lanes >= v * ncond, lanes < (v + 1) * ncond)
        result = jnp.where(keep, moved, result)
    out_ref[...] = result[:, :cols]
    every.wait_send()


def shards(npb, nwa, psi_val, psi_cond, trials, screened, kmap):
    klocal, nval, pts = psi_val.shape
    ncond = psi_cond.shape[1]
    cols = trials.shape[1]
    kcount, points, n = klocal * nwa, pts * npb, npb * nwa
    ntrial = cols * npb // (nval * ncond)
    nrows = screened.shape[1]
    nx = 2 if npb % 4 == 0 else 1
    nz = npb // (2 * nx)
    g = math.gcd(klocal, LANES // pts)
    vmem = pl.BlockSpec(memory_space=pltpu.VMEM)
    smem = pl.BlockSpec(memory_space=pltpu.SMEM)
    anywhere = pl.BlockSpec(memory_space=pl.ANY)
    prow = up(klocal // g * (nval + ncond) + klocal, PACK)
    r = cols // ncond
    crows = up(ncond, PACK)
    pairs = nval * nval
    wide = ncond * pairs
    width = points // 2
    block = math.gcd(kcount, max(1, 256 // pairs))
    kpad = up(klocal, 8)
    dims = (npb, nwa, klocal, nval, ncond, pts, cols, ntrial, nrows, nx, nz, g)
    dma = pltpu.SemaphoreType.DMA
    return pl.pallas_call(
        functools.partial(kernel, dims),
        out_shape=jax.ShapeDtypeStruct((klocal, cols), F32),
        in_specs=[smem] + [anywhere] * 4, out_specs=vmem,
        scratch_shapes=[
            pltpu.VMEM(psi_val.shape, BF16),
            pltpu.VMEM(psi_cond.shape, BF16),
            pltpu.VMEM(trials.shape, BF16),
            pltpu.VMEM((prow, LANES), F32),
            pltpu.VMEM((nrows, points), BF16),
            pltpu.VMEM((n, prow, LANES), BF16),
            pltpu.VMEM((kcount, nval, points), F32),
            pltpu.VMEM((kcount, crows, width), F32),
            pltpu.VMEM((nwa * ntrial * kpad, LANES), F32),
            pltpu.VMEM((LANES, wide), BF16),
            pltpu.VMEM((wide // LANES, nwa * ntrial * kpad, LANES), F32),
            pltpu.VMEM((kcount, ncond * crows, points), BF16),
            pltpu.VMEM((kcount // block, block * pairs, nrows), F32),
            pltpu.VMEM((kcount, 2 * pairs, points), BF16),
            pltpu.VMEM((kcount, 2 * crows, wide), BF16),
            pltpu.VMEM((kcount, crows * crows, LANES), F32),
            pltpu.VMEM((kcount, 2 * crows, nval * ntrial), F32),
            pltpu.VMEM((nwa, nval * ntrial, LANES), F32),
            pltpu.VMEM((n, r, LANES), F32),
            pltpu.VMEM((n, r, LANES), F32),
            pltpu.SMEM((kcount,), jnp.int32),
            dma((3,)), dma, dma((nz,)), dma((nz,)), dma((nz,)), dma, dma, dma, dma,
        ],
        compiler_params=pltpu.CompilerParams(
            collective_id=0, has_side_effects=True, vmem_limit_bytes=44 * 1024 * 1024),
        name="bethe",
    )(kmap, psi_val, psi_cond, trials, screened)


def solution(mesh):
    in_specs = (
        P("wa", None, "pb"),
        P("wa", None, "pb"),
        P("wa", "pb"),
        P("pb", "wa", None),
        P("pb", None),
    )
    body = functools.partial(shards, mesh.shape["pb"], mesh.shape["wa"])
    return jax.shard_map(body, mesh=mesh, in_specs=in_specs, out_specs=P("wa", "pb"), check_vma=False)
```

```python
import functools
import math

import jax
import jax.numpy as jnp
from jax import lax
from jax.experimental import pallas as pl
from jax.experimental.pallas import tpu as pltpu
from jax.sharding import PartitionSpec as P

MESH = pl.DeviceIdType.MESH
LANES = 128
PACK = 16
F32 = jnp.float32
BF16 = jnp.bfloat16
NT = (((1,), (1,)), ((), ()))


def up(value, unit):
    return -(-value // unit) * unit


def flip(value, j):
    bit = 1
    while bit <= j:
        if j & bit:
            value = value + bit - 2 * bit * lax.rem(value // bit, 2)
        bit *= 2
    return value


def kernel(dims, kmap_hbm, val_hbm, cond_hbm, tri_hbm, w_hbm, out_ref,
           sval, scond, turned_ref, stri, pack_ref, w_ref, slots, val_ref, cond_ref, tri_ref, spread_ref, xt_ref,
           b_ref, sum_ref, right_ref, gh_ref, h_ref, res_ref, turn_ref, part_ref, rslots, kmap_ref, inv_ref,
           load_sem, w_sem, line_sem, quad_sem, core_sem, hop_send, core_send, give_send, give_recv):
    npb, nwa, klocal, nval, ncond, pts, cols, ntrial, nrows, nx, nz, g = dims
    kcount, points, n = klocal * nwa, pts * npb, npb * nwa
    quads = nx * nwa
    kk_count = klocal // g
    per = LANES // pts
    pairs = nval * nval
    crows = cond_ref.shape[1]
    high = ncond // 8 * 8
    low = ncond - high
    r = cols // ncond
    spread = nval // r
    width = points // 2
    deep = nz // 2
    pb, wa = lax.axis_index("pb"), lax.axis_index("wa")
    me = wa * npb + pb
    core, px, pz = lax.rem(pb, 2), lax.rem(pb // 2, nx), pb // (2 * nx)

    def device(z, x, y, c):
        return (z * nx + x) * 2 + c, y

    def there(z, x, y):
        return flip(pz, z), lax.rem(px + x, nx), lax.rem(wa + y, nwa)

    def source(z, x, y):
        return flip(pz, z), lax.rem(px - x + nx, nx), lax.rem(wa - y + nwa, nwa)

    def slot(z, x, y):
        return slots.at[(z * 2 + core) * quads + x * nwa + y]

    others = [(x, y) for x in range(nx) for y in range(nwa) if (x, y) != (0, 0)]
    near = list(range(1, nz // 2))
    far = list(range(nz // 2, nz))
    straight = [(0, x, y) for x, y in others] + [(z, 0, 0) for z in near + far]
    straight += [(z, x, y) for z in near for x, y in others]
    twin = device(pz, px, wa, 1 - core)

    barrier = pltpu.get_barrier_semaphore()
    for place in straight:
        pl.semaphore_signal(barrier, inc=1, device_id=device(*there(*place), core), device_id_type=MESH)
    pl.semaphore_signal(barrier, inc=1, device_id=twin, device_id_type=MESH)

    loads = [pltpu.make_async_copy(val_hbm, sval, load_sem.at[0]),
             pltpu.make_async_copy(cond_hbm, scond, load_sem.at[1]),
             pltpu.make_async_copy(tri_hbm, stri, load_sem.at[2])]
    for load in loads:
        load.start()
    kload = pltpu.make_async_copy(kmap_hbm, kmap_ref, load_sem.at[3])
    kload.start()
    wload = pltpu.make_async_copy(w_hbm.at[0], w_ref, w_sem)
    wload.start()
    for load in loads:
        load.wait()

    def beside(pieces):
        have = sum(piece.shape[1] for piece in pieces)
        if have < LANES:
            pieces = pieces + [jnp.zeros((pieces[0].shape[0], LANES - have), F32)]
        return jnp.concatenate(pieces, axis=1) if len(pieces) > 1 else pieces[0]

    kpad = up(klocal, 8)
    for c in range(ncond):
        turned_ref[c * kpad:c * kpad + klocal, :] = beside([scond[c].astype(F32)])
    for i in range(kk_count):
        pack_ref[i * nval:(i + 1) * nval, :] = beside([sval[j * kk_count + i].astype(F32) for j in range(g)])
        base = kk_count * nval + i * ncond
        pack_ref[base:base + ncond, :] = beside(
            [turned_ref[pl.ds(j * kk_count + i, ncond, stride=kpad), :][:, :pts] for j in range(g)])
    base = kk_count * (nval + ncond)
    pack_ref[base:base + klocal, :] = beside([stri[...].astype(F32)])
    if base + klocal < pack_ref.shape[0]:
        pack_ref[base + klocal:, :] = jnp.zeros((pack_ref.shape[0] - base - klocal, LANES), F32)
    slots[(pz * 2 + core) * quads + px * nwa + wa] = pack_ref[...].astype(BF16)

    def copy(held, to, send, recv):
        return pltpu.make_async_remote_copy(
            src_ref=slot(*held), dst_ref=slot(*held), send_sem=send, recv_sem=recv, device_id=to, device_id_type=MESH)

    def wait_for(blocks, send, recv):
        span = slots.at[pl.ds(0, blocks)]
        return pltpu.make_async_remote_copy(
            src_ref=span, dst_ref=span, send_sem=send, recv_sem=recv, device_id=twin, device_id_type=MESH)

    own = source(0, 0, 0)
    pl.semaphore_wait(barrier, len(straight) + 1)
    for z in far:
        copy(own, device(*there(z, 0, 0), core), hop_send, line_sem.at[z]).start()
    for x, y in others:
        copy(own, device(*there(0, x, y), core), hop_send, quad_sem.at[0]).start()
    for z in near:
        for x, y in [(0, 0)] + others:
            copy(own, device(*there(z, x, y), core), hop_send, quad_sem.at[z]).start()
    copy(own, twin, core_send, core_sem.at[0]).start()

    kload.wait()
    for k in range(kcount):
        found = jnp.int32(0)
        for j in range(kcount):
            found = jnp.where(kmap_ref[0, j] == k, j, found)
        inv_ref[k] = found
    tri_ref[...] = jnp.zeros_like(tri_ref)
    for k in range(kcount):
        h_ref[k, ncond * ncond:, :] = jnp.zeros((h_ref.shape[1] - ncond * ncond, LANES), F32)
        right_ref[k, 0:pairs, :] = jnp.zeros((pairs, points), BF16)
    wide = ncond * pairs
    lane = lax.broadcasted_iota(jnp.int32, (LANES, wide), 1)
    row = lax.broadcasted_iota(jnp.int32, (LANES, wide), 0)
    spread_ref[...] = jnp.where(lax.rem(lane, nval) * ncond + lane // pairs == row, 1.0, 0.0).astype(BF16)
    wload.wait()

    def across(z, places):
        for x, y in places:
            copy(source(z, x, y), twin, core_send, core_sem.at[z]).start()

    for z in far:
        copy(source(z, 0, 0), device(*there(z, 0, 0), core), hop_send, line_sem.at[z]).wait_recv()
        for x, y in others:
            copy(source(z, 0, 0), device(*there(0, x, y), core), hop_send, quad_sem.at[z]).start()
        across(z, [(0, 0)])
    if others:
        wait_for(len(others), hop_send, quad_sem.at[0]).wait_recv()
        across(0, others)
    for z in near:
        wait_for(quads, hop_send, quad_sem.at[z]).wait_recv()
        across(z, [(0, 0)] + others)

    def far_quads(z):
        if others:
            wait_for(len(others), hop_send, quad_sem.at[z]).wait_recv()
            across(z, others)

    def arrived(z):
        wait_for(quads, core_send, core_sem.at[z]).wait_recv()

    lane_group = lax.broadcasted_iota(jnp.int32, (slots.shape[1], LANES), 1) // pts
    trials_here = deep * nx * 2 // spread

    def unpack(side):
        for w in range(nwa):
            rows = [None] * trials_here
            for t in range(width // LANES):
                at = slice(t * LANES, (t + 1) * LANES)
                whole_at = pl.ds(pl.multiple_of(side * width + t * LANES, LANES), LANES)
                blocks = []
                for i in range(t * per, (t + 1) * per):
                    z, x, c = side * deep + i // (nx * 2), i // 2 % nx, i % 2
                    blocks.append(slots[(z * 2 + c) * quads + x * nwa + w].astype(F32))
                    base = kk_count * (nval + ncond)
                    piece = blocks[-1][base:base + klocal]
                    shift = i % spread * cols
                    piece = pltpu.roll(piece, shift, 1) if shift else piece
                    held = rows[i // spread]
                    rows[i // spread] = piece if held is None else held + piece
                for j in range(g):
                    whole = None
                    for i in range(per):
                        shift = (i - j) * pts % LANES
                        moved = pltpu.roll(blocks[i], shift, 1) if shift else blocks[i]
                        whole = moved if whole is None else jnp.where(lane_group == i, moved, whole)
                    for kk in range(kk_count):
                        k = w * klocal + j * kk_count + kk
                        val_ref[k, :, whole_at] = whole[kk * nval:(kk + 1) * nval]
                        base = kk_count * nval + kk * ncond
                        cond_ref[k, 0:ncond, at] = whole[base:base + ncond]
                        for i in range(ncond, crows, max(low, 1)):
                            cond_ref[k, i:i + low, at] = whole[base + high:base + ncond]
            start = pl.multiple_of((w * ntrial + side * trials_here) * kpad, 8)
            for i in range(trials_here):
                tri_ref[pl.ds(start + i * kpad, klocal), :] = rows[i]
            x = tri_ref[pl.ds(start, trials_here * kpad), :].astype(BF16)
            x = jnp.dot(x, spread_ref[...], preferred_element_type=F32)
            for t in range(wide // LANES):
                xt_ref[t, pl.ds(start, trials_here * kpad), :] = x[:, t * LANES:(t + 1) * LANES]

    local = pl.ds(pl.multiple_of(wa * nrows, nrows), nrows)
    half = lax.broadcasted_iota(jnp.int32, (crows, LANES), 1) < pairs
    half_tile = lax.broadcasted_iota(jnp.int32, (8, LANES), 1) < pairs
    first = lax.broadcasted_iota(jnp.int32, (8, LANES), 0) < low
    block = math.gcd(kcount, max(1, 512 // pairs))

    def products(one, two, at):
        parts = []
        mate = val_ref[two, :, at]
        for v in range(0, nval, 2):
            both = jnp.concatenate([val_ref[one, v:v + 1, at] * mate, val_ref[one, v + 1:v + 2, at] * mate], axis=0)
            parts.append(both.astype(BF16))
        return jnp.concatenate(parts, axis=0)

    def build(k, side):
        p = kmap_ref[0, k]
        for t in range(width // LANES):
            tile = slice(t * LANES, (t + 1) * LANES)
            to = pl.ds(pl.multiple_of(side * width + t * LANES, LANES), LANES)
            here = cond_ref[k, 0:high, tile]
            for d in range(0, ncond, 2):
                two = [here * cond_ref[p, d + i:d + i + 1, tile] for i in range(2)]
                b_ref[k, d * high:(d + 2) * high, to] = jnp.concatenate(two, axis=0).astype(BF16)
            here = cond_ref[k, high:crows, tile]
            for d in range(0, ncond, 4):
                mates = [cond_ref[p, d + i:d + i + 1, tile] for i in range(4)]
                two = [here * jnp.where(first, mates[0], mates[1]), here * jnp.where(first, mates[2], mates[3])]
                base = ncond * high + d * low
                b_ref[k, base:base + 4 * low, to] = jnp.concatenate(two, axis=0).astype(BF16)

    def rows_of(b, side):
        whole = []
        for i in range(block):
            k = b * block + i
            whole.append(jnp.concatenate(
                [products(k, kmap_ref[0, k], pl.ds(pl.multiple_of(side * width + t, LANES), LANES))
                 for t in range(0, width, LANES)], axis=1))
        at = pl.ds(pl.multiple_of(side * width, LANES), width)
        return lax.dot_general(jnp.concatenate(whole, axis=0), w_ref[:, at], NT, preferred_element_type=F32)

    def early(side):
        unpack(side)

        def step(b, carry):
            sum_ref[b] = rows_of(b, side)
            for i in range(block):
                build(b * block + i, side)
            return carry

        lax.fori_loop(0, kcount // block, step, 0, unroll=2)

    def late(side):
        unpack(side)

        def step(b, carry):
            left = (sum_ref[b] + rows_of(b, side)).astype(BF16)
            whole = []
            for i in range(block):
                k = b * block + i
                right_ref[k, 0:pairs, local] = left[i * pairs:(i + 1) * pairs]
                whole.append(jnp.concatenate(
                    [products(kmap_ref[0, k], k, pl.ds(pl.multiple_of(wa * nrows + t, LANES), LANES))
                     for t in range(0, nrows, LANES)], axis=1))
                build(k, side)
            turned = jnp.dot(jnp.concatenate(whole, axis=0), w_ref[...], preferred_element_type=F32).astype(BF16)
            for i in range(block):
                right_ref[b * block + i, pairs:2 * pairs, :] = turned[i * pairs:(i + 1) * pairs]
            return carry

        lax.fori_loop(0, kcount // block, step, 0, unroll=2)

        def one_k(k, carry):
            both = lax.dot_general(b_ref[k], right_ref[k], NT, preferred_element_type=F32)
            h_ref[k, 0:ncond * ncond] = both
            more = ncond * high
            h_parts = [h_ref[k, pl.ds(c, crows, stride=high), :] for c in range(high)]
            h_parts += [h_ref[k, pl.ds(more + c, crows, stride=low), :] for c in range(low)]
            for d in range(0, ncond, 2):
                at = slice(d * pairs, (d + 2) * pairs)
                top = jnp.where(half_tile, both[d * high:(d + 1) * high],
                                pltpu.roll(both[(d + 1) * high:(d + 2) * high], pairs, 1))
                rest = both[more + d * low:more + (d + 2) * low]
                rest = jnp.where(half_tile, rest, pltpu.roll(pltpu.roll(rest, pairs, 1), low, 0))
                gh_ref[k, 0:crows, at] = jnp.concatenate([top, rest], axis=0).astype(BF16)
                gh_ref[k, crows:, at] = jnp.where(half, pltpu.roll(h_parts[d], pairs, 1), h_parts[d + 1]).astype(BF16)
            return carry

        lax.fori_loop(0, kcount, one_k, 0, unroll=math.gcd(kcount, 16))

    side = pz // deep
    for z in [0] + near:
        arrived(z)
    early(side)
    for z in far:
        far_quads(z)
    for z in far:
        arrived(z)
    late(1 - side)

    which = lax.rem(lax.broadcasted_iota(jnp.int32, (ntrial, wide), 1) // nval, nval)
    spots = [jnp.where(which == v, 1.0, 0.0).astype(BF16) for v in range(nval)]

    def one_p(p, carry):
        w, kl = p // klocal, lax.rem(p, klocal)
        x = jnp.concatenate([xt_ref[t, pl.ds(w * ntrial * kpad + kl, ntrial, stride=kpad), :]
                             for t in range(wide // LANES)], axis=1).astype(BF16)
        x = jnp.concatenate([x * spots[v] for v in range(nval)], axis=0)
        both = jnp.concatenate([gh_ref[inv_ref[p], 0:crows], gh_ref[p, crows:2 * crows]], axis=0)
        res_ref[p] = lax.dot_general(both, x, NT, preferred_element_type=F32)
        return carry

    lax.fori_loop(0, kcount, one_p, 0, unroll=math.gcd(kcount, 16))

    def give(to, mine):
        return pltpu.make_async_remote_copy(
            src_ref=part_ref.at[to], dst_ref=rslots.at[mine], send_sem=give_send, recv_sem=give_recv,
            device_id=(lax.rem(to, npb), to // npb), device_id_type=MESH)

    for w in range(nwa):
        rows = [res_ref[kmap_ref[0, k], 0:crows] + res_ref[inv_ref[k], crows:2 * crows]
                for k in reversed(range(w * klocal, (w + 1) * klocal))]
        if klocal * crows < LANES:
            rows.append(jnp.zeros((LANES - klocal * crows, nval * ntrial), F32))
        turn_ref[w] = jnp.concatenate(rows, axis=0).T
        for i in range(npb):
            s, v0 = i * r // nval, i * r % nval
            part_ref[w * npb + i] = turn_ref[w, pl.ds(v0 * ntrial + s, r, stride=ntrial), :]
    rslots[me] = part_ref[me]

    def send(j, carry):
        give(lax.rem(me + j, n), me).start()
        return carry

    lax.fori_loop(1, n, send, 0)
    every = pltpu.make_async_remote_copy(
        src_ref=part_ref.at[pl.ds(0, n - 1)], dst_ref=rslots.at[pl.ds(0, n - 1)], send_sem=give_send,
        recv_sem=give_recv, device_id=twin, device_id_type=MESH)
    wait_for(len(straight) + len(far) * len(others), hop_send, line_sem.at[0]).wait_send()
    wait_for(nz * quads, core_send, line_sem.at[0]).wait_send()
    every.wait_recv()
    total = jnp.sum(rslots[...], axis=0)
    lanes = lax.broadcasted_iota(jnp.int32, (klocal, LANES), 1)
    result = jnp.zeros((klocal, LANES), F32)
    for v in range(r):
        shift = (v * ncond - (klocal - 1) * crows) % LANES
        moved = pltpu.roll(jnp.broadcast_to(total[v:v + 1], (klocal, LANES)), 0, 1, stride=crows, stride_axis=0)
        moved = pltpu.roll(moved, shift, 1) if shift else moved
        keep = jnp.logical_and(lanes >= v * ncond, lanes < (v + 1) * ncond)
        result = jnp.where(keep, moved, result)
    out_ref[...] = result[:, :cols]
    every.wait_send()


def shards(npb, nwa, psi_val, psi_cond, trials, screened, kmap):
    klocal, nval, pts = psi_val.shape
    ncond = psi_cond.shape[1]
    cols = trials.shape[1]
    kcount, points, n = klocal * nwa, pts * npb, npb * nwa
    ntrial = cols * npb // (nval * ncond)
    nrows = screened.shape[1]
    nx = 2 if npb % 4 == 0 else 1
    nz = npb // (2 * nx)
    g = math.gcd(klocal, LANES // pts)
    vmem = pl.BlockSpec(memory_space=pltpu.VMEM)
    anywhere = pl.BlockSpec(memory_space=pl.ANY)
    prow = up(klocal // g * (nval + ncond) + klocal, PACK)
    r = cols // ncond
    crows = up(ncond, PACK)
    pairs = nval * nval
    wide = ncond * pairs
    width = points // 2
    block = math.gcd(kcount, max(1, 512 // pairs))
    kpad = up(klocal, 8)
    dims = (npb, nwa, klocal, nval, ncond, pts, cols, ntrial, nrows, nx, nz, g)
    dma = pltpu.SemaphoreType.DMA
    return pl.pallas_call(
        functools.partial(kernel, dims),
        out_shape=jax.ShapeDtypeStruct((klocal, cols), F32),
        in_specs=[anywhere] * 5, out_specs=vmem,
        scratch_shapes=[
            pltpu.VMEM(psi_val.shape, BF16),
            pltpu.VMEM((ncond, klocal, pts), BF16),
            pltpu.VMEM((ncond * kpad, LANES), F32),
            pltpu.VMEM(trials.shape, BF16),
            pltpu.VMEM((prow, LANES), F32),
            pltpu.VMEM((nrows, points), BF16),
            pltpu.VMEM((n, prow, LANES), BF16),
            pltpu.VMEM((kcount, nval, points), F32),
            pltpu.VMEM((kcount, crows, width), F32),
            pltpu.VMEM((nwa * ntrial * kpad, LANES), F32),
            pltpu.VMEM((LANES, wide), BF16),
            pltpu.VMEM((wide // LANES, nwa * ntrial * kpad, LANES), F32),
            pltpu.VMEM((kcount, ncond * ncond, points), BF16),
            pltpu.VMEM((kcount // block, block * pairs, nrows), F32),
            pltpu.VMEM((kcount, 2 * pairs, points), BF16),
            pltpu.VMEM((kcount, 2 * crows, wide), BF16),
            pltpu.VMEM((kcount, ncond // 8 * 8 * ncond + ncond % 8 * crows, LANES), F32),
            pltpu.VMEM((kcount, 2 * crows, nval * ntrial), F32),
            pltpu.VMEM((nwa, nval * ntrial, LANES), F32),
            pltpu.VMEM((n, r, LANES), F32),
            pltpu.VMEM((n, r, LANES), F32),
            pltpu.SMEM(kmap.shape, jnp.int32),
            pltpu.SMEM((kcount,), jnp.int32),
            dma((4,)), dma, dma((nz,)), dma((nz,)), dma((nz,)), dma, dma, dma, dma,
        ],
        compiler_params=pltpu.CompilerParams(
            collective_id=0, has_side_effects=True, vmem_limit_bytes=63 * 1024 * 1024),
        name="bethe",
    )(kmap, psi_val, psi_cond.transpose(1, 0, 2), trials, screened)


def solution(mesh):
    in_specs = (
        P("wa", None, "pb"),
        P("wa", None, "pb"),
        P("wa", "pb"),
        P("pb", "wa", None),
        P("pb", None),
    )
    body = functools.partial(shards, mesh.shape["pb"], mesh.shape["wa"])
    return jax.shard_map(body, mesh=mesh, in_specs=in_specs, out_specs=P("wa", "pb"), check_vma=False)
```

```python
import functools
import math

import jax
import jax.numpy as jnp
from jax import lax
from jax.experimental import pallas as pl
from jax.experimental.pallas import tpu as pltpu
from jax.sharding import PartitionSpec as P

MESH = pl.DeviceIdType.MESH
LANES = 128
PACK = 16
F32 = jnp.float32
BF16 = jnp.bfloat16
NT = (((1,), (1,)), ((), ()))


def up(value, unit):
    return -(-value // unit) * unit


def flip(value, j):
    bit = 1
    while bit <= j:
        if j & bit:
            value = value + bit - 2 * bit * lax.rem(value // bit, 2)
        bit *= 2
    return value


def kernel(dims, kmap_hbm, val_hbm, cond_hbm, tri_hbm, w_hbm, out_ref,
           sval, scond, turned_ref, stri, pack_ref, w_ref, slots, val_ref, cond_ref, tri_ref, spread_ref, xt_ref,
           b_ref, sum_ref, right_ref, gh_ref, h_ref, res_ref, turn_ref, part_ref, rslots, kmap_ref, inv_ref,
           load_sem, w_sem, line_sem, quad_sem, core_sem, hop_send, core_send, give_send, give_recv):
    npb, nwa, klocal, nval, ncond, pts, cols, ntrial, nrows, nx, nz, g = dims
    kcount, points, n = klocal * nwa, pts * npb, npb * nwa
    quads = nx * nwa
    kk_count = klocal // g
    per = LANES // pts
    pairs = nval * nval
    crows = cond_ref.shape[1]
    high = ncond // 8 * 8
    low = ncond - high
    r = cols // ncond
    spread = nval // r
    width = points // 2
    deep = nz // 2
    pb, wa = lax.axis_index("pb"), lax.axis_index("wa")
    me = wa * npb + pb
    core, px, pz = lax.rem(pb, 2), lax.rem(pb // 2, nx), pb // (2 * nx)

    def device(z, x, y, c):
        return (z * nx + x) * 2 + c, y

    def there(z, x, y):
        return flip(pz, z), lax.rem(px + x, nx), lax.rem(wa + y, nwa)

    def source(z, x, y):
        return flip(pz, z), lax.rem(px - x + nx, nx), lax.rem(wa - y + nwa, nwa)

    def slot(z, x, y):
        return slots.at[(z * 2 + core) * quads + x * nwa + y]

    others = [(x, y) for x in range(nx) for y in range(nwa) if (x, y) != (0, 0)]
    near = list(range(1, nz // 2))
    far = list(range(nz // 2, nz))
    around = [(0, x, y) for x, y in others] + [(z, x, y) for z in near for x, y in [(0, 0)] + others]
    straight = around + [(deep, 0, 0)]
    twin = device(pz, px, wa, 1 - core)

    barrier = pltpu.get_barrier_semaphore()
    for place in straight:
        pl.semaphore_signal(barrier, inc=1, device_id=device(*there(*place), core), device_id_type=MESH)
    pl.semaphore_signal(barrier, inc=1, device_id=twin, device_id_type=MESH)

    loads = [pltpu.make_async_copy(val_hbm, sval, load_sem.at[0]),
             pltpu.make_async_copy(cond_hbm, scond, load_sem.at[1]),
             pltpu.make_async_copy(tri_hbm, stri, load_sem.at[2])]
    for load in loads:
        load.start()
    kload = pltpu.make_async_copy(kmap_hbm, kmap_ref, load_sem.at[3])
    kload.start()
    wload = pltpu.make_async_copy(w_hbm.at[0], w_ref, w_sem)
    wload.start()
    for load in loads:
        load.wait()

    def beside(pieces):
        have = sum(piece.shape[1] for piece in pieces)
        if have < LANES:
            pieces = pieces + [jnp.zeros((pieces[0].shape[0], LANES - have), F32)]
        return jnp.concatenate(pieces, axis=1) if len(pieces) > 1 else pieces[0]

    kpad = up(klocal, 8)
    for c in range(ncond):
        turned_ref[c * kpad:c * kpad + klocal, :] = beside([scond[c].astype(F32)])
    for i in range(kk_count):
        pack_ref[i * nval:(i + 1) * nval, :] = beside([sval[j * kk_count + i].astype(F32) for j in range(g)])
        base = kk_count * nval + i * ncond
        pack_ref[base:base + ncond, :] = beside(
            [turned_ref[pl.ds(j * kk_count + i, ncond, stride=kpad), :][:, :pts] for j in range(g)])
    base = kk_count * (nval + ncond)
    pack_ref[base:base + klocal, :] = beside([stri[...].astype(F32)])
    if base + klocal < pack_ref.shape[0]:
        pack_ref[base + klocal:, :] = jnp.zeros((pack_ref.shape[0] - base - klocal, LANES), F32)
    slots[(pz * 2 + core) * quads + px * nwa + wa] = pack_ref[...].astype(BF16)

    def copy(held, to, send, recv):
        return pltpu.make_async_remote_copy(
            src_ref=slot(*held), dst_ref=slot(*held), send_sem=send, recv_sem=recv, device_id=to, device_id_type=MESH)

    def wait_for(blocks, send, recv):
        span = slots.at[pl.ds(0, blocks)]
        return pltpu.make_async_remote_copy(
            src_ref=span, dst_ref=span, send_sem=send, recv_sem=recv, device_id=twin, device_id_type=MESH)

    own = source(0, 0, 0)
    pl.semaphore_wait(barrier, len(straight) + 1)
    copy(own, device(*there(deep, 0, 0), core), hop_send, line_sem).start()
    for z, x, y in reversed(around):
        copy(own, device(*there(z, x, y), core), hop_send, quad_sem.at[z]).start()
    copy(own, twin, core_send, core_sem.at[0]).start()

    kload.wait()
    for k in range(kcount):
        found = jnp.int32(0)
        for j in range(kcount):
            found = jnp.where(kmap_ref[0, j] == k, j, found)
        inv_ref[k] = found
    tri_ref[...] = jnp.zeros_like(tri_ref)
    for k in range(kcount):
        h_ref[k, ncond * ncond:, :] = jnp.zeros((h_ref.shape[1] - ncond * ncond, LANES), F32)
        right_ref[k, 0:pairs, :] = jnp.zeros((pairs, points), BF16)
    wide = ncond * pairs
    lane = lax.broadcasted_iota(jnp.int32, (LANES, wide), 1)
    row = lax.broadcasted_iota(jnp.int32, (LANES, wide), 0)
    spread_ref[...] = jnp.where(lax.rem(lane, nval) * ncond + lane // pairs == row, 1.0, 0.0).astype(BF16)
    wload.wait()

    def across(z, places):
        for x, y in places:
            copy(source(z, x, y), twin, core_send, core_sem.at[z]).start()

    held = source(deep, 0, 0)
    copy(held, device(*there(deep, 0, 0), core), hop_send, line_sem).wait_recv()
    for z, x, y in reversed(around):
        copy(held, device(*there(z, x, y), core), hop_send, quad_sem.at[deep + z]).start()
    across(deep, [(0, 0)])
    if others:
        wait_for(len(others), hop_send, quad_sem.at[0]).wait_recv()
        across(0, others)
    for z in near:
        wait_for(quads, hop_send, quad_sem.at[z]).wait_recv()
        across(z, [(0, 0)] + others)

    def far_quads(z):
        fresh = others if z == deep else [(0, 0)] + others
        if fresh:
            wait_for(len(fresh), hop_send, quad_sem.at[z]).wait_recv()
            across(z, fresh)

    def arrived(z):
        wait_for(quads, core_send, core_sem.at[z]).wait_recv()

    lane_group = lax.broadcasted_iota(jnp.int32, (slots.shape[1], LANES), 1) // pts
    trials_here = deep * nx * 2 // spread

    def unpack(side):
        for w in range(nwa):
            rows = [None] * trials_here
            for t in range(width // LANES):
                at = slice(t * LANES, (t + 1) * LANES)
                whole_at = pl.ds(pl.multiple_of(side * width + t * LANES, LANES), LANES)
                blocks = []
                for i in range(t * per, (t + 1) * per):
                    z, x, c = side * deep + i // (nx * 2), i // 2 % nx, i % 2
                    blocks.append(slots[(z * 2 + c) * quads + x * nwa + w].astype(F32))
                    base = kk_count * (nval + ncond)
                    piece = blocks[-1][base:base + klocal]
                    shift = i % spread * cols
                    piece = pltpu.roll(piece, shift, 1) if shift else piece
                    held = rows[i // spread]
                    rows[i // spread] = piece if held is None else held + piece
                for j in range(g):
                    whole = None
                    for i in range(per):
                        shift = (i - j) * pts % LANES
                        moved = pltpu.roll(blocks[i], shift, 1) if shift else blocks[i]
                        whole = moved if whole is None else jnp.where(lane_group == i, moved, whole)
                    for kk in range(kk_count):
                        k = w * klocal + j * kk_count + kk
                        val_ref[k, :, whole_at] = whole[kk * nval:(kk + 1) * nval]
                        base = kk_count * nval + kk * ncond
                        cond_ref[k, 0:ncond, at] = whole[base:base + ncond]
                        for i in range(ncond, crows, max(low, 1)):
                            cond_ref[k, i:i + low, at] = whole[base + high:base + ncond]
            start = pl.multiple_of((w * ntrial + side * trials_here) * kpad, 8)
            for i in range(trials_here):
                tri_ref[pl.ds(start + i * kpad, klocal), :] = rows[i]
            x = tri_ref[pl.ds(start, trials_here * kpad), :].astype(BF16)
            x = jnp.dot(x, spread_ref[...], preferred_element_type=F32)
            for t in range(wide // LANES):
                xt_ref[t, pl.ds(start, trials_here * kpad), :] = x[:, t * LANES:(t + 1) * LANES]

    local = pl.ds(pl.multiple_of(wa * nrows, nrows), nrows)
    half = lax.broadcasted_iota(jnp.int32, (crows, LANES), 1) < pairs
    half_tile = lax.broadcasted_iota(jnp.int32, (8, LANES), 1) < pairs
    first = lax.broadcasted_iota(jnp.int32, (8, LANES), 0) < low
    block = math.gcd(kcount, max(1, 512 // pairs))

    def products(one, two, at):
        parts = []
        mate = val_ref[two, :, at]
        for v in range(0, nval, 2):
            both = jnp.concatenate([val_ref[one, v:v + 1, at] * mate, val_ref[one, v + 1:v + 2, at] * mate], axis=0)
            parts.append(both.astype(BF16))
        return jnp.concatenate(parts, axis=0)

    def build(k, side):
        p = kmap_ref[0, k]
        for t in range(width // LANES):
            tile = slice(t * LANES, (t + 1) * LANES)
            to = pl.ds(pl.multiple_of(side * width + t * LANES, LANES), LANES)
            here = cond_ref[k, 0:high, tile]
            for d in range(0, ncond, 2):
                two = [here * cond_ref[p, d + i:d + i + 1, tile] for i in range(2)]
                b_ref[k, d * high:(d + 2) * high, to] = jnp.concatenate(two, axis=0).astype(BF16)
            here = cond_ref[k, high:crows, tile]
            for d in range(0, ncond, 4):
                mates = [cond_ref[p, d + i:d + i + 1, tile] for i in range(4)]
                two = [here * jnp.where(first, mates[0], mates[1]), here * jnp.where(first, mates[2], mates[3])]
                base = ncond * high + d * low
                b_ref[k, base:base + 4 * low, to] = jnp.concatenate(two, axis=0).astype(BF16)

    def rows_of(b, side):
        whole = []
        for i in range(block):
            k = b * block + i
            whole.append(jnp.concatenate(
                [products(k, kmap_ref[0, k], pl.ds(pl.multiple_of(side * width + t, LANES), LANES))
                 for t in range(0, width, LANES)], axis=1))
        at = pl.ds(pl.multiple_of(side * width, LANES), width)
        return lax.dot_general(jnp.concatenate(whole, axis=0), w_ref[:, at], NT, preferred_element_type=F32)

    def early(side):
        unpack(side)

        def step(b, carry):
            sum_ref[b] = rows_of(b, side)
            for i in range(block):
                build(b * block + i, side)
            return carry

        lax.fori_loop(0, kcount // block, step, 0, unroll=2)

    def late(side):
        unpack(side)

        def step(b, carry):
            left = (sum_ref[b] + rows_of(b, side)).astype(BF16)
            whole = []
            for i in range(block):
                k = b * block + i
                right_ref[k, 0:pairs, local] = left[i * pairs:(i + 1) * pairs]
                whole.append(jnp.concatenate(
                    [products(kmap_ref[0, k], k, pl.ds(pl.multiple_of(wa * nrows + t, LANES), LANES))
                     for t in range(0, nrows, LANES)], axis=1))
                build(k, side)
            turned = jnp.dot(jnp.concatenate(whole, axis=0), w_ref[...], preferred_element_type=F32).astype(BF16)
            for i in range(block):
                right_ref[b * block + i, pairs:2 * pairs, :] = turned[i * pairs:(i + 1) * pairs]
            return carry

        lax.fori_loop(0, kcount // block, step, 0, unroll=2)

        def one_k(k, carry):
            both = lax.dot_general(b_ref[k], right_ref[k], NT, preferred_element_type=F32)
            h_ref[k, 0:ncond * ncond] = both
            more = ncond * high
            h_parts = [h_ref[k, pl.ds(c, crows, stride=high), :] for c in range(high)]
            h_parts += [h_ref[k, pl.ds(more + c, crows, stride=low), :] for c in range(low)]
            for d in range(0, ncond, 2):
                at = slice(d * pairs, (d + 2) * pairs)
                top = jnp.where(half_tile, both[d * high:(d + 1) * high],
                                pltpu.roll(both[(d + 1) * high:(d + 2) * high], pairs, 1))
                rest = both[more + d * low:more + (d + 2) * low]
                rest = jnp.where(half_tile, rest, pltpu.roll(pltpu.roll(rest, pairs, 1), low, 0))
                gh_ref[k, 0:crows, at] = jnp.concatenate([top, rest], axis=0).astype(BF16)
                gh_ref[k, crows:, at] = jnp.where(half, pltpu.roll(h_parts[d], pairs, 1), h_parts[d + 1]).astype(BF16)
            return carry

        lax.fori_loop(0, kcount, one_k, 0, unroll=math.gcd(kcount, 16))

    side = pz // deep
    for z in [0] + near:
        arrived(z)
    early(side)
    for z in far:
        far_quads(z)
    for z in far:
        arrived(z)
    late(1 - side)

    which = lax.rem(lax.broadcasted_iota(jnp.int32, (ntrial, wide), 1) // nval, nval)
    spots = [jnp.where(which == v, 1.0, 0.0).astype(BF16) for v in range(nval)]

    def one_p(p, carry):
        w, kl = p // klocal, lax.rem(p, klocal)
        x = jnp.concatenate([xt_ref[t, pl.ds(w * ntrial * kpad + kl, ntrial, stride=kpad), :]
                             for t in range(wide // LANES)], axis=1).astype(BF16)
        x = jnp.concatenate([x * spots[v] for v in range(nval)], axis=0)
        both = jnp.concatenate([gh_ref[inv_ref[p], 0:crows], gh_ref[p, crows:2 * crows]], axis=0)
        res_ref[p] = lax.dot_general(both, x, NT, preferred_element_type=F32)
        return carry

    lax.fori_loop(0, kcount, one_p, 0, unroll=math.gcd(kcount, 16))

    def give(to, mine):
        return pltpu.make_async_remote_copy(
            src_ref=part_ref.at[to], dst_ref=rslots.at[mine], send_sem=give_send, recv_sem=give_recv,
            device_id=(lax.rem(to, npb), to // npb), device_id_type=MESH)

    for w in range(nwa):
        rows = [res_ref[kmap_ref[0, k], 0:crows] + res_ref[inv_ref[k], crows:2 * crows]
                for k in reversed(range(w * klocal, (w + 1) * klocal))]
        if klocal * crows < LANES:
            rows.append(jnp.zeros((LANES - klocal * crows, nval * ntrial), F32))
        turn_ref[w] = jnp.concatenate(rows, axis=0).T
        for i in range(npb):
            s, v0 = i * r // nval, i * r % nval
            part_ref[w * npb + i] = turn_ref[w, pl.ds(v0 * ntrial + s, r, stride=ntrial), :]

        def send(j, carry, w=w):
            to = lax.rem(pb + j, npb)

            @pl.when(jnp.logical_or(to != pb, wa != w))
            def go():
                give(w * npb + to, me).start()
            return carry

        lax.fori_loop(0, npb, send, 0)
    rslots[me] = part_ref[me]
    every = pltpu.make_async_remote_copy(
        src_ref=part_ref.at[pl.ds(0, n - 1)], dst_ref=rslots.at[pl.ds(0, n - 1)], send_sem=give_send,
        recv_sem=give_recv, device_id=twin, device_id_type=MESH)
    wait_for(len(straight) + len(around), hop_send, line_sem).wait_send()
    wait_for(nz * quads, core_send, line_sem).wait_send()
    every.wait_recv()
    total = jnp.sum(rslots[...], axis=0)
    lanes = lax.broadcasted_iota(jnp.int32, (klocal, LANES), 1)
    result = jnp.zeros((klocal, LANES), F32)
    for v in range(r):
        shift = (v * ncond - (klocal - 1) * crows) % LANES
        moved = pltpu.roll(jnp.broadcast_to(total[v:v + 1], (klocal, LANES)), 0, 1, stride=crows, stride_axis=0)
        moved = pltpu.roll(moved, shift, 1) if shift else moved
        keep = jnp.logical_and(lanes >= v * ncond, lanes < (v + 1) * ncond)
        result = jnp.where(keep, moved, result)
    out_ref[...] = result[:, :cols]
    every.wait_send()


def shards(npb, nwa, psi_val, psi_cond, trials, screened, kmap):
    klocal, nval, pts = psi_val.shape
    ncond = psi_cond.shape[1]
    cols = trials.shape[1]
    kcount, points, n = klocal * nwa, pts * npb, npb * nwa
    ntrial = cols * npb // (nval * ncond)
    nrows = screened.shape[1]
    nx = 2 if npb % 4 == 0 else 1
    nz = npb // (2 * nx)
    g = math.gcd(klocal, LANES // pts)
    vmem = pl.BlockSpec(memory_space=pltpu.VMEM)
    anywhere = pl.BlockSpec(memory_space=pl.ANY)
    prow = up(klocal // g * (nval + ncond) + klocal, PACK)
    r = cols // ncond
    crows = up(ncond, PACK)
    pairs = nval * nval
    wide = ncond * pairs
    width = points // 2
    block = math.gcd(kcount, max(1, 512 // pairs))
    kpad = up(klocal, 8)
    dims = (npb, nwa, klocal, nval, ncond, pts, cols, ntrial, nrows, nx, nz, g)
    dma = pltpu.SemaphoreType.DMA
    return pl.pallas_call(
        functools.partial(kernel, dims),
        out_shape=jax.ShapeDtypeStruct((klocal, cols), F32),
        in_specs=[anywhere] * 5, out_specs=vmem,
        scratch_shapes=[
            pltpu.VMEM(psi_val.shape, BF16),
            pltpu.VMEM((ncond, klocal, pts), BF16),
            pltpu.VMEM((ncond * kpad, LANES), F32),
            pltpu.VMEM(trials.shape, BF16),
            pltpu.VMEM((prow, LANES), F32),
            pltpu.VMEM((nrows, points), BF16),
            pltpu.VMEM((n, prow, LANES), BF16),
            pltpu.VMEM((kcount, nval, points), F32),
            pltpu.VMEM((kcount, crows, width), F32),
            pltpu.VMEM((nwa * ntrial * kpad, LANES), F32),
            pltpu.VMEM((LANES, wide), BF16),
            pltpu.VMEM((wide // LANES, nwa * ntrial * kpad, LANES), F32),
            pltpu.VMEM((kcount, ncond * ncond, points), BF16),
            pltpu.VMEM((kcount // block, block * pairs, nrows), F32),
            pltpu.VMEM((kcount, 2 * pairs, points), BF16),
            pltpu.VMEM((kcount, 2 * crows, wide), BF16),
            pltpu.VMEM((kcount, ncond // 8 * 8 * ncond + ncond % 8 * crows, LANES), F32),
            pltpu.VMEM((kcount, 2 * crows, nval * ntrial), F32),
            pltpu.VMEM((nwa, nval * ntrial, LANES), F32),
            pltpu.VMEM((n, r, LANES), F32),
            pltpu.VMEM((n, r, LANES), F32),
            pltpu.SMEM(kmap.shape, jnp.int32),
            pltpu.SMEM((kcount,), jnp.int32),
            dma((4,)), dma, dma, dma((nz,)), dma((nz,)), dma, dma, dma, dma,
        ],
        compiler_params=pltpu.CompilerParams(
            collective_id=0, has_side_effects=True, vmem_limit_bytes=63 * 1024 * 1024),
        name="bethe",
    )(kmap, psi_val, psi_cond.transpose(1, 0, 2), trials, screened)


def solution(mesh):
    in_specs = (
        P("wa", None, "pb"),
        P("wa", None, "pb"),
        P("wa", "pb"),
        P("pb", "wa", None),
        P("pb", None),
    )
    body = functools.partial(shards, mesh.shape["pb"], mesh.shape["wa"])
    return jax.shard_map(body, mesh=mesh, in_specs=in_specs, out_specs=P("wa", "pb"), check_vma=False)
```

```python
import functools
import math

import jax
import jax.numpy as jnp
from jax import lax
from jax.experimental import pallas as pl
from jax.experimental.pallas import tpu as pltpu
from jax.sharding import PartitionSpec as P

MESH = pl.DeviceIdType.MESH
LANES = 128
PACK = 16
F32 = jnp.float32
BF16 = jnp.bfloat16
NT = (((1,), (1,)), ((), ()))


def up(value, unit):
    return -(-value // unit) * unit


def flip(value, j):
    bit = 1
    while bit <= j:
        if j & bit:
            value = value + bit - 2 * bit * lax.rem(value // bit, 2)
        bit *= 2
    return value


def kernel(dims, kmap_hbm, val_hbm, cond_hbm, tri_hbm, w_hbm, out_ref,
           sval, scond, turned_ref, stri, pack_ref, w_ref, slots, val_ref, cond_ref, tri_ref, spread_ref, xt_ref,
           b_ref, sum_ref, right_ref, gh_ref, h_ref, res_ref, turn_ref, part_ref, rslots, kmap_ref, inv_ref,
           load_sem, w_sem, line_sem, quad_sem, core_sem, hop_send, core_send, give_send, give_recv):
    npb, nwa, klocal, nval, ncond, pts, cols, ntrial, nrows, nx, nz, g = dims
    kcount, points, n = klocal * nwa, pts * npb, npb * nwa
    quads = nx * nwa
    kk_count = klocal // g
    per = LANES // pts
    pairs = nval * nval
    crows = cond_ref.shape[1]
    high = ncond // 8 * 8
    low = ncond - high
    r = cols // ncond
    spread = nval // r
    width = points // 2
    deep = nz // 2
    pb, wa = lax.axis_index("pb"), lax.axis_index("wa")
    me = wa * npb + pb
    core, px, pz = lax.rem(pb, 2), lax.rem(pb // 2, nx), pb // (2 * nx)

    def device(z, x, y, c):
        return (z * nx + x) * 2 + c, y

    def there(z, x, y):
        return flip(pz, z), lax.rem(px + x, nx), lax.rem(wa + y, nwa)

    def source(z, x, y):
        return flip(pz, z), lax.rem(px - x + nx, nx), lax.rem(wa - y + nwa, nwa)

    def slot(z, x, y):
        return slots.at[(z * 2 + core) * quads + x * nwa + y]

    others = [(x, y) for x in range(nx) for y in range(nwa) if (x, y) != (0, 0)]
    near = list(range(1, nz // 2))
    far = list(range(nz // 2, nz))
    around = [(0, x, y) for x, y in others] + [(z, x, y) for z in near for x, y in [(0, 0)] + others]
    straight = around + [(deep, 0, 0)]
    twin = device(pz, px, wa, 1 - core)

    barrier = pltpu.get_barrier_semaphore()
    for place in straight:
        pl.semaphore_signal(barrier, inc=1, device_id=device(*there(*place), core), device_id_type=MESH)
    pl.semaphore_signal(barrier, inc=1, device_id=twin, device_id_type=MESH)

    loads = [pltpu.make_async_copy(val_hbm, sval, load_sem.at[0]),
             pltpu.make_async_copy(cond_hbm, scond, load_sem.at[1]),
             pltpu.make_async_copy(tri_hbm, stri, load_sem.at[2])]
    for load in loads:
        load.start()
    kload = pltpu.make_async_copy(kmap_hbm, kmap_ref, load_sem.at[3])
    kload.start()
    wload = pltpu.make_async_copy(w_hbm.at[0], w_ref, w_sem)
    wload.start()
    for load in loads:
        load.wait()

    def beside(pieces):
        have = sum(piece.shape[1] for piece in pieces)
        if have < LANES:
            pieces = pieces + [jnp.zeros((pieces[0].shape[0], LANES - have), F32)]
        return jnp.concatenate(pieces, axis=1) if len(pieces) > 1 else pieces[0]

    kpad = up(klocal, 8)
    for c in range(ncond):
        turned_ref[c * kpad:c * kpad + klocal, :] = beside([scond[c].astype(F32)])
    for i in range(kk_count):
        pack_ref[i * nval:(i + 1) * nval, :] = beside([sval[j * kk_count + i].astype(F32) for j in range(g)])
        base = kk_count * nval + i * ncond
        pack_ref[base:base + ncond, :] = beside(
            [turned_ref[pl.ds(j * kk_count + i, ncond, stride=kpad), :][:, :pts] for j in range(g)])
    base = kk_count * (nval + ncond)
    pack_ref[base:base + klocal, :] = beside([stri[...].astype(F32)])
    if base + klocal < pack_ref.shape[0]:
        pack_ref[base + klocal:, :] = jnp.zeros((pack_ref.shape[0] - base - klocal, LANES), F32)
    slots[(pz * 2 + core) * quads + px * nwa + wa] = pack_ref[...].astype(BF16)

    def copy(held, to, send, recv):
        return pltpu.make_async_remote_copy(
            src_ref=slot(*held), dst_ref=slot(*held), send_sem=send, recv_sem=recv, device_id=to, device_id_type=MESH)

    def wait_for(blocks, send, recv):
        span = slots.at[pl.ds(0, blocks)]
        return pltpu.make_async_remote_copy(
            src_ref=span, dst_ref=span, send_sem=send, recv_sem=recv, device_id=twin, device_id_type=MESH)

    own = source(0, 0, 0)
    pl.semaphore_wait(barrier, len(straight) + 1)
    copy(own, device(*there(deep, 0, 0), core), hop_send, line_sem).start()
    for z, x, y in reversed(around):
        copy(own, device(*there(z, x, y), core), hop_send, quad_sem.at[z]).start()
    copy(own, twin, core_send, core_sem.at[0]).start()

    kload.wait()
    for k in range(kcount):
        found = jnp.int32(0)
        for j in range(kcount):
            found = jnp.where(kmap_ref[0, j] == k, j, found)
        inv_ref[k] = found
    tri_ref[...] = jnp.zeros_like(tri_ref)
    for k in range(kcount):
        h_ref[k, ncond * ncond:, :] = jnp.zeros((h_ref.shape[1] - ncond * ncond, LANES), F32)
        right_ref[k, 0:pairs, :] = jnp.zeros((pairs, points), BF16)
    wide = ncond * pairs
    lane = lax.broadcasted_iota(jnp.int32, (LANES, wide), 1)
    row = lax.broadcasted_iota(jnp.int32, (LANES, wide), 0)
    spread_ref[...] = jnp.where(lax.rem(lane, nval) * ncond + lane // pairs == row, 1.0, 0.0).astype(BF16)
    wload.wait()

    def across(z, places):
        for x, y in places:
            copy(source(z, x, y), twin, core_send, core_sem.at[z]).start()

    held = source(deep, 0, 0)
    copy(held, device(*there(deep, 0, 0), core), hop_send, line_sem).wait_recv()
    for z, x, y in reversed(around):
        copy(held, device(*there(z, x, y), core), hop_send, quad_sem.at[deep + z]).start()
    across(deep, [(0, 0)])
    if others:
        wait_for(len(others), hop_send, quad_sem.at[0]).wait_recv()
        across(0, others)
    for z in near:
        wait_for(quads, hop_send, quad_sem.at[z]).wait_recv()
        across(z, [(0, 0)] + others)

    def far_quads(z):
        fresh = others if z == deep else [(0, 0)] + others
        if fresh:
            wait_for(len(fresh), hop_send, quad_sem.at[z]).wait_recv()
            across(z, fresh)

    def arrived(z):
        wait_for(quads, core_send, core_sem.at[z]).wait_recv()

    lane_group = lax.broadcasted_iota(jnp.int32, (slots.shape[1], LANES), 1) // pts
    trials_here = deep * nx * 2 // spread

    def unpack(side):
        for w in range(nwa):
            rows = [None] * trials_here
            for t in range(width // LANES):
                at = slice(t * LANES, (t + 1) * LANES)
                whole_at = pl.ds(pl.multiple_of(side * width + t * LANES, LANES), LANES)
                blocks = []
                for i in range(t * per, (t + 1) * per):
                    z, x, c = side * deep + i // (nx * 2), i // 2 % nx, i % 2
                    blocks.append(slots[(z * 2 + c) * quads + x * nwa + w].astype(F32))
                    base = kk_count * (nval + ncond)
                    piece = blocks[-1][base:base + klocal]
                    shift = i % spread * cols
                    piece = pltpu.roll(piece, shift, 1) if shift else piece
                    held = rows[i // spread]
                    rows[i // spread] = piece if held is None else held + piece
                for j in range(g):
                    whole = None
                    for i in range(per):
                        shift = (i - j) * pts % LANES
                        moved = pltpu.roll(blocks[i], shift, 1) if shift else blocks[i]
                        whole = moved if whole is None else jnp.where(lane_group == i, moved, whole)
                    for kk in range(kk_count):
                        k = w * klocal + j * kk_count + kk
                        val_ref[k, :, whole_at] = whole[kk * nval:(kk + 1) * nval]
                        base = kk_count * nval + kk * ncond
                        cond_ref[k, 0:ncond, at] = whole[base:base + ncond]
                        for i in range(ncond, crows, max(low, 1)):
                            cond_ref[k, i:i + low, at] = whole[base + high:base + ncond]
            start = pl.multiple_of((w * ntrial + side * trials_here) * kpad, 8)
            for i in range(trials_here):
                tri_ref[pl.ds(start + i * kpad, klocal), :] = rows[i]
            x = tri_ref[pl.ds(start, trials_here * kpad), :].astype(BF16)
            x = jnp.dot(x, spread_ref[...], preferred_element_type=F32)
            for t in range(wide // LANES):
                xt_ref[t, pl.ds(start, trials_here * kpad), :] = x[:, t * LANES:(t + 1) * LANES]

    local = pl.ds(pl.multiple_of(wa * nrows, nrows), nrows)
    half = lax.broadcasted_iota(jnp.int32, (crows, LANES), 1) < pairs
    half_tile = lax.broadcasted_iota(jnp.int32, (8, LANES), 1) < pairs
    first = lax.broadcasted_iota(jnp.int32, (8, LANES), 0) < low
    block = math.gcd(kcount, max(1, 512 // pairs))

    def products(one, two, at):
        parts = []
        mate = val_ref[two, :, at]
        for v in range(0, nval, 2):
            both = jnp.concatenate([val_ref[one, v:v + 1, at] * mate, val_ref[one, v + 1:v + 2, at] * mate], axis=0)
            parts.append(both.astype(BF16))
        return jnp.concatenate(parts, axis=0)

    def build(k, side):
        p = kmap_ref[0, k]
        for t in range(width // LANES):
            tile = slice(t * LANES, (t + 1) * LANES)
            to = pl.ds(pl.multiple_of(side * width + t * LANES, LANES), LANES)
            here = cond_ref[k, 0:high, tile]
            for d in range(0, ncond, 2):
                two = [here * cond_ref[p, d + i:d + i + 1, tile] for i in range(2)]
                b_ref[k, d * high:(d + 2) * high, to] = jnp.concatenate(two, axis=0).astype(BF16)
            here = cond_ref[k, high:crows, tile]
            for d in range(0, ncond, 4):
                mates = [cond_ref[p, d + i:d + i + 1, tile] for i in range(4)]
                two = [here * jnp.where(first, mates[0], mates[1]), here * jnp.where(first, mates[2], mates[3])]
                base = ncond * high + d * low
                b_ref[k, base:base + 4 * low, to] = jnp.concatenate(two, axis=0).astype(BF16)

    def rows_of(b, side):
        whole = []
        for i in range(block):
            k = b * block + i
            whole.append(jnp.concatenate(
                [products(k, kmap_ref[0, k], pl.ds(pl.multiple_of(side * width + t, LANES), LANES))
                 for t in range(0, width, LANES)], axis=1))
        at = pl.ds(pl.multiple_of(side * width, LANES), width)
        return lax.dot_general(jnp.concatenate(whole, axis=0), w_ref[:, at], NT, preferred_element_type=F32)

    def early(side):
        unpack(side)

        def step(b, carry):
            sum_ref[b] = rows_of(b, side)
            for i in range(block):
                build(b * block + i, side)
            return carry

        lax.fori_loop(0, kcount // block, step, 0, unroll=2)

    def late(side):
        unpack(side)

        def step(b, carry):
            left = (sum_ref[b] + rows_of(b, side)).astype(BF16)
            whole = []
            for i in range(block):
                k = b * block + i
                right_ref[k, 0:pairs, local] = left[i * pairs:(i + 1) * pairs]
                whole.append(jnp.concatenate(
                    [products(kmap_ref[0, k], k, pl.ds(pl.multiple_of(wa * nrows + t, LANES), LANES))
                     for t in range(0, nrows, LANES)], axis=1))
                build(k, side)
            turned = jnp.dot(jnp.concatenate(whole, axis=0), w_ref[...], preferred_element_type=F32).astype(BF16)
            for i in range(block):
                right_ref[b * block + i, pairs:2 * pairs, :] = turned[i * pairs:(i + 1) * pairs]
            return carry

        lax.fori_loop(0, kcount // block, step, 0, unroll=2)

        def one_k(k, carry):
            both = lax.dot_general(b_ref[k], right_ref[k], NT, preferred_element_type=F32)
            h_ref[k, 0:ncond * ncond] = both
            more = ncond * high
            h_parts = [h_ref[k, pl.ds(c, crows, stride=high), :] for c in range(high)]
            h_parts += [h_ref[k, pl.ds(more + c, crows, stride=low), :] for c in range(low)]
            for d in range(0, ncond, 2):
                at = slice(d * pairs, (d + 2) * pairs)
                top = jnp.where(half_tile, both[d * high:(d + 1) * high],
                                pltpu.roll(both[(d + 1) * high:(d + 2) * high], pairs, 1))
                rest = both[more + d * low:more + (d + 2) * low]
                rest = jnp.where(half_tile, rest, pltpu.roll(pltpu.roll(rest, pairs, 1), low, 0))
                gh_ref[k, 0:crows, at] = jnp.concatenate([top, rest], axis=0).astype(BF16)
                gh_ref[k, crows:, at] = jnp.where(half, pltpu.roll(h_parts[d], pairs, 1), h_parts[d + 1]).astype(BF16)
            return carry

        lax.fori_loop(0, kcount, one_k, 0, unroll=math.gcd(kcount, 16))

    side = pz // deep
    for z in [0] + near:
        arrived(z)
    early(side)
    for z in reversed(far):
        far_quads(z)
    for z in far:
        arrived(z)
    late(1 - side)

    which = lax.rem(lax.broadcasted_iota(jnp.int32, (ntrial, wide), 1) // nval, nval)
    spots = [jnp.where(which == v, 1.0, 0.0).astype(BF16) for v in range(nval)]

    def one_p(p, carry):
        w, kl = p // klocal, lax.rem(p, klocal)
        x = jnp.concatenate([xt_ref[t, pl.ds(w * ntrial * kpad + kl, ntrial, stride=kpad), :]
                             for t in range(wide // LANES)], axis=1).astype(BF16)
        x = jnp.concatenate([x * spots[v] for v in range(nval)], axis=0)
        both = jnp.concatenate([gh_ref[inv_ref[p], 0:crows], gh_ref[p, crows:2 * crows]], axis=0)
        res_ref[p] = lax.dot_general(both, x, NT, preferred_element_type=F32)
        return carry

    lax.fori_loop(0, kcount, one_p, 0, unroll=math.gcd(kcount, 16))

    def give(to, mine):
        return pltpu.make_async_remote_copy(
            src_ref=part_ref.at[to], dst_ref=rslots.at[mine], send_sem=give_send, recv_sem=give_recv,
            device_id=(lax.rem(to, npb), to // npb), device_id_type=MESH)

    for w in range(nwa):
        rows = [res_ref[kmap_ref[0, k], 0:crows] + res_ref[inv_ref[k], crows:2 * crows]
                for k in reversed(range(w * klocal, (w + 1) * klocal))]
        if klocal * crows < LANES:
            rows.append(jnp.zeros((LANES - klocal * crows, nval * ntrial), F32))
        turn_ref[w] = jnp.concatenate(rows, axis=0).T
        for i in range(npb):
            s, v0 = i * r // nval, i * r % nval
            part_ref[w * npb + i] = turn_ref[w, pl.ds(v0 * ntrial + s, r, stride=ntrial), :]

        def send(j, carry, w=w):
            to = lax.rem(pb + j, npb)

            @pl.when(jnp.logical_or(to != pb, wa != w))
            def go():
                give(w * npb + to, me).start()
            return carry

        lax.fori_loop(0, npb, send, 0)
    rslots[me] = part_ref[me]
    every = pltpu.make_async_remote_copy(
        src_ref=part_ref.at[pl.ds(0, n - 1)], dst_ref=rslots.at[pl.ds(0, n - 1)], send_sem=give_send,
        recv_sem=give_recv, device_id=twin, device_id_type=MESH)
    wait_for(len(straight) + len(around), hop_send, line_sem).wait_send()
    wait_for(nz * quads, core_send, line_sem).wait_send()
    every.wait_recv()
    total = jnp.sum(rslots[...], axis=0)
    lanes = lax.broadcasted_iota(jnp.int32, (klocal, LANES), 1)
    result = jnp.zeros((klocal, LANES), F32)
    for v in range(r):
        shift = (v * ncond - (klocal - 1) * crows) % LANES
        moved = pltpu.roll(jnp.broadcast_to(total[v:v + 1], (klocal, LANES)), 0, 1, stride=crows, stride_axis=0)
        moved = pltpu.roll(moved, shift, 1) if shift else moved
        keep = jnp.logical_and(lanes >= v * ncond, lanes < (v + 1) * ncond)
        result = jnp.where(keep, moved, result)
    out_ref[...] = result[:, :cols]
    every.wait_send()


def shards(npb, nwa, psi_val, psi_cond, trials, screened, kmap):
    klocal, nval, pts = psi_val.shape
    ncond = psi_cond.shape[1]
    cols = trials.shape[1]
    kcount, points, n = klocal * nwa, pts * npb, npb * nwa
    ntrial = cols * npb // (nval * ncond)
    nrows = screened.shape[1]
    nx = 2 if npb % 4 == 0 else 1
    nz = npb // (2 * nx)
    g = math.gcd(klocal, LANES // pts)
    vmem = pl.BlockSpec(memory_space=pltpu.VMEM)
    anywhere = pl.BlockSpec(memory_space=pl.ANY)
    prow = up(klocal // g * (nval + ncond) + klocal, PACK)
    r = cols // ncond
    crows = up(ncond, PACK)
    pairs = nval * nval
    wide = ncond * pairs
    width = points // 2
    block = math.gcd(kcount, max(1, 512 // pairs))
    kpad = up(klocal, 8)
    dims = (npb, nwa, klocal, nval, ncond, pts, cols, ntrial, nrows, nx, nz, g)
    dma = pltpu.SemaphoreType.DMA
    return pl.pallas_call(
        functools.partial(kernel, dims),
        out_shape=jax.ShapeDtypeStruct((klocal, cols), F32),
        in_specs=[anywhere] * 5, out_specs=vmem,
        scratch_shapes=[
            pltpu.VMEM(psi_val.shape, BF16),
            pltpu.VMEM((ncond, klocal, pts), BF16),
            pltpu.VMEM((ncond * kpad, LANES), F32),
            pltpu.VMEM(trials.shape, BF16),
            pltpu.VMEM((prow, LANES), F32),
            pltpu.VMEM((nrows, points), BF16),
            pltpu.VMEM((n, prow, LANES), BF16),
            pltpu.VMEM((kcount, nval, points), F32),
            pltpu.VMEM((kcount, crows, width), F32),
            pltpu.VMEM((nwa * ntrial * kpad, LANES), F32),
            pltpu.VMEM((LANES, wide), BF16),
            pltpu.VMEM((wide // LANES, nwa * ntrial * kpad, LANES), F32),
            pltpu.VMEM((kcount, ncond * ncond, points), BF16),
            pltpu.VMEM((kcount // block, block * pairs, nrows), F32),
            pltpu.VMEM((kcount, 2 * pairs, points), BF16),
            pltpu.VMEM((kcount, 2 * crows, wide), BF16),
            pltpu.VMEM((kcount, ncond // 8 * 8 * ncond + ncond % 8 * crows, LANES), F32),
            pltpu.VMEM((kcount, 2 * crows, nval * ntrial), F32),
            pltpu.VMEM((nwa, nval * ntrial, LANES), F32),
            pltpu.VMEM((n, r, LANES), F32),
            pltpu.VMEM((n, r, LANES), F32),
            pltpu.SMEM(kmap.shape, jnp.int32),
            pltpu.SMEM((kcount,), jnp.int32),
            dma((4,)), dma, dma, dma((nz,)), dma((nz,)), dma, dma, dma, dma,
        ],
        compiler_params=pltpu.CompilerParams(
            collective_id=0, has_side_effects=True, vmem_limit_bytes=63 * 1024 * 1024),
        name="bethe",
    )(kmap, psi_val, psi_cond.transpose(1, 0, 2), trials, screened)


def solution(mesh):
    in_specs = (
        P("wa", None, "pb"),
        P("wa", None, "pb"),
        P("wa", "pb"),
        P("pb", "wa", None),
        P("pb", None),
    )
    body = functools.partial(shards, mesh.shape["pb"], mesh.shape["wa"])
    return jax.shard_map(body, mesh=mesh, in_specs=in_specs, out_specs=P("wa", "pb"), check_vma=False)
```
